32 devices in a mesh: row: 4 (over y, core), col: 8 (over z, x).
Axes of the slice: x: 2, y: 2, z: 4, core: 2. Of those that a mesh axis runs over, the one named last changes fastest.
Arguments:
- tokens: bfloat16 [4096, 4096], P(('row', 'col')), may hold values from -6 to 6
- expert_ids: int32 [4096, 8], P(('row', 'col')), may hold values from 0 to 31, all different within a row; in each aligned block of 128 rows (0 to 127, 128 to 255, ...) at most 40 rows name the same one
- router_weight: bfloat16 [4096, 32], replicated, may hold values from -0.09375 to 0.09375
- w_gate: bfloat16 [32, 4096, 768], P(('row', 'col')), may hold values from -0.09375 to 0.09375
- w_up: bfloat16 [32, 4096, 768], P(('row', 'col')), may hold values from -0.09375 to 0.09375
- w_down: bfloat16 [32, 768, 4096], P(('row', 'col')), may hold values from -0.21875 to 0.21875
Outputs:
- mixed: bfloat16 [4096, 4096], P(('row', 'col'))
The draws below stay inside these ranges and needn't reach their ends.
Inputs may be any that keep to these rules, and one draw needn't show every extreme that they name: `expert_ids`: each row names 8 different experts; among the rows of one device no expert is named more than 40 times, a bound that some block reaches.
All inputs are finite; a program needn't handle non-finite values.
Results may differ from the reference program's by a relative error of at most 0.0059.
Values may be sent and summed in bfloat16 or wider, within the bound.
A program may use at most 128 MiB of HBM per device.

```python
import math
import jax
import jax.numpy as jnp
import numpy as np
from jax import lax

D = 4096
FFW = 768
TOP = 8
TOK_DEV = 128
EXPERTS = 32
MOST = 40
TOKENS = 4096
N_ROW = 4
N_COL = 8


def block_levels(key, extent, pieces, low, top_value):
    loudness, own = 1.0, jax.random.fold_in(key, 6)
    for dim, blocks in pieces:
        draws = jnp.exp(jax.random.uniform(jax.random.fold_in(own, dim), (blocks,), jnp.float32, low / len(pieces), top_value / len(pieces)))
        loudness = loudness * jnp.repeat(draws, extent[dim] // blocks).reshape([-1 if axis == dim else 1 for axis in range(len(extent))])
    return loudness


def routed_block(key, own, number, rows, count, top, bound, slope):
    ranking = jax.random.permutation(key, count)
    heavy_load, ordinary = shares(count, rows * top, bound, slope, True), shares(count, rows * top, bound, slope, False)
    places = jnp.arange(count)

    def named(lengths, offset_by):
        used = int((lengths > 0).sum())
        fixed = max(1, used // 4)
        passed = fixed + (places - fixed + offset_by * (used - fixed)) % max(1, count - fixed)
        return jnp.zeros((count,), jnp.int32).at[ranking[jnp.where(places < fixed, places, passed)]].set(jnp.asarray(lengths, jnp.int32))

    lengths = jnp.where(number % 4 == 0, named(heavy_load, number // 4), named(ordinary, number - number // 4 - 1))
    mixed = jax.random.permutation(jax.random.fold_in(own, 3), count)
    donor, taker = mixed[0:count // 2 * 2:2], mixed[1:count // 2 * 2:2]
    slack = jnp.minimum(lengths[donor] - 1, bound - lengths[taker]) // 2
    slack = jnp.where((donor == ranking[0]) | (taker == ranking[0]) | (lengths[taker] == 0), 0, jnp.maximum(slack, 0))
    passed = jax.random.randint(jax.random.fold_in(own, 4), (count // 2,), 0, 1 << 20) % (slack + 1)
    lengths = lengths.at[donor].add(-passed).at[taker].add(passed)
    labels = jnp.searchsorted(jnp.cumsum(lengths), jnp.arange(rows * top), side="right").astype(jnp.int32)
    table = labels.reshape(top, rows).T
    table = table[jax.random.permutation(jax.random.fold_in(own, 1), rows)]
    offset_by = jax.random.randint(jax.random.fold_in(own, 2), (rows, 1), 0, top)
    return jnp.take_along_axis(table, (jnp.arange(top)[None, :] + offset_by) % top, axis=1)


def shares(number_of, total, most, slope, full):
    portions = [(1 << 20) // math.isqrt(rank ** slope) + 1 for rank in range(1, number_of + 1)]
    largest = most if full else min(most, max(-(-total // number_of), total * portions[0] // sum(portions)))
    least = 1 if total - largest >= number_of - 1 else 0
    given, spare = [largest] + [least] * (number_of - 1), total - largest - least * (number_of - 1)
    while spare > 0:
        free = [i for i in range(1, number_of) if given[i] < largest] or [i for i in range(1, number_of) if given[i] < most]
        pool, budget = sum([portions[i] for i in free]), spare
        for i in free:
            addition = min(most - given[i], max(1, budget * portions[i] // pool), spare)
            given[i] = given[i] + addition
            spare = spare - addition
    return np.array(given)


def noise(stream_key, dims, spread, most, pieces=(), kind=jnp.bfloat16):
    drawn = spread * jax.random.normal(stream_key, dims, jnp.float32)
    if pieces:
        drawn = drawn * block_levels(stream_key, dims, pieces, -0.22, 0.18)
    return jnp.clip(drawn, -most, most).astype(kind)


def setup_inputs(seed: int = 0) -> dict:
    key_of = jax.random.split(jax.random.key(seed), 7)
    tokens = noise(key_of[0], (TOKENS, D), 1.0, 6.0, ((0, 32),))
    expert_ids_keys = jax.random.split(jax.random.fold_in(key_of[1], 1), TOKENS // TOK_DEV)
    expert_ids_turns = jax.random.permutation(jax.random.fold_in(key_of[1], 3), TOKENS // TOK_DEV)
    expert_ids = jax.vmap(lambda own, number: routed_block(jax.random.fold_in(key_of[1], 2), own, number, TOK_DEV, EXPERTS, TOP, MOST, 2))(expert_ids_keys, expert_ids_turns).reshape((TOKENS, TOP))
    router_weight = noise(key_of[2], (D, EXPERTS), D ** -0.5, 0.09375)
    w_gate = noise(key_of[3], (EXPERTS, D, FFW), D ** -0.5, 0.09375, ((0, 32),))
    w_up = noise(key_of[4], (EXPERTS, D, FFW), D ** -0.5, 0.09375, ((0, 32),))
    w_down = noise(key_of[5], (EXPERTS, FFW, D), FFW ** -0.5, 0.21875, ((0, 32),))
    return {"tokens": tokens, "expert_ids": expert_ids, "router_weight": router_weight, "w_gate": w_gate, "w_up": w_up, "w_down": w_down}


def reference(tokens, expert_ids, router_weight, w_gate, w_up, w_down):
    tok_count = tokens.shape[0]
    dev_count = N_ROW * N_COL
    logits = jnp.dot(tokens, router_weight, preferred_element_type=jnp.float32)
    chosen = jnp.take_along_axis(logits, expert_ids, axis=1)
    scores = jnp.exp(chosen)
    gate_vals = scores / jnp.sum(scores, axis=1, keepdims=True)
    flat_ids = expert_ids.reshape(dev_count, TOK_DEV * TOP)
    onehot = (flat_ids[:, :, None] == jnp.arange(EXPERTS, dtype=jnp.int32)[None, None, :]).astype(jnp.int32)
    earlier = jnp.cumsum(onehot, axis=1) - onehot
    slot_pos = jnp.sum(earlier * onehot, axis=2)
    dev_index = jnp.arange(dev_count, dtype=jnp.int32)[:, None]
    position = (flat_ids * (dev_count * MOST) + dev_index * MOST + slot_pos).reshape(-1)
    tok_index = (dev_index * TOK_DEV + jnp.arange(TOK_DEV * TOP, dtype=jnp.int32)[None, :] // TOP).reshape(-1)
    table = jnp.full((EXPERTS * dev_count * MOST,), tok_count, jnp.int32).at[position].set(tok_index)
    table = table.reshape(EXPERTS, dev_count * MOST)
    gate_table = jnp.zeros((EXPERTS * dev_count * MOST,), jnp.float32).at[position].set(gate_vals.reshape(-1))
    gate_table = gate_table.reshape(EXPERTS, dev_count * MOST)

    def one_expert(total, items):
        rows_idx, gate_row, gate_mat, up_mat, down_mat = items
        rows = jnp.take(tokens, rows_idx, axis=0, mode="fill", fill_value=0)
        gate_part = jnp.dot(rows, gate_mat, preferred_element_type=jnp.float32)
        up_part = jnp.dot(rows, up_mat, preferred_element_type=jnp.float32)
        hidden = (jax.nn.silu(gate_part) * up_part).astype(jnp.bfloat16)
        expert_out = jnp.dot(hidden, down_mat, preferred_element_type=jnp.float32).astype(jnp.bfloat16)
        total = total.at[rows_idx].add(gate_row[:, None] * expert_out.astype(jnp.float32), mode="drop")
        return total, None

    total = jnp.zeros((tok_count, D), jnp.float32)
    total, _ = lax.scan(one_expert, total, (table, gate_table, w_gate, w_up, w_down))
    return total.astype(jnp.bfloat16)
```

```python
import functools

import jax
import jax.numpy as jnp
from jax import lax
from jax.experimental import pallas as pl
from jax.experimental.pallas import tpu as pltpu
from jax.sharding import PartitionSpec as P

MESH = pl.DeviceIdType.MESH
DEEP = 4
PIECES = 2
CB = 0


def flip(index, step):
    bit = step & 1
    if bit:
        index = index + 1 - 2 * (index % 2)
    if step & 2:
        index = index + 2 - 4 * ((index // 2) % 2)
    return index


def moe_kernel(dims, tok_ref, tab_ref, wg_hbm, wu_hbm, wd_hbm, out_ref, *refs):
    rows_axis, side, pad, resident = dims
    far = None if resident else refs[0]
    (tokbuf, tabbuf, stage, xbuf, hid, near, psend, precv, own, wg, wu, wd,
     wsem, tok_send, tok_recv, tab_send, tab_recv, x_send, x_recv,
     r_send, r_recv, p_send, p_recv, l_sem) = refs if resident else refs[1:]
    back = near if resident else far
    plane = rows_axis * side
    tokens, width = tok_ref.shape
    ffw = wg.shape[1]
    part = width // PIECES
    row = lax.axis_index("row")
    col = lax.axis_index("col")
    deep = col // side
    across = col % side
    me = row * side + across
    rest = pl.ds(0, (plane - 1) * pad)

    def slot_of(other):
        return pl.ds(pl.multiple_of(other * pad, 8), pad)

    def peer_id(other):
        return (other // side, deep * side + other % side)

    def partner(j):
        if plane & (plane - 1):
            return (me + j) % plane
        return sum(bit * ((me // bit + j // bit) % 2) for bit in (1 << i for i in range(plane.bit_length() - 1)))

    def deep_id(step):
        return (row, flip(deep, step) * side + across)

    barrier = pltpu.get_barrier_semaphore()

    @pl.loop(1, plane)
    def _(j):
        pl.semaphore_signal(barrier, inc=1, device_id=peer_id((me + j) % plane), device_id_type=MESH)

    for step in range(1, DEEP):
        pl.semaphore_signal(barrier, inc=1, device_id=deep_id(step), device_id_type=MESH)

    weights = [pltpu.make_async_copy(src.at[0], dst, wsem.at[i])
               for i, (src, dst) in enumerate(((wg_hbm, wg), (wu_hbm, wu), (wd_hbm, wd)))]
    for copy in weights:
        copy.start()
    pl.semaphore_wait(barrier, plane - 1 + DEEP - 1)

    def tab_copy(step):
        return pltpu.make_async_remote_copy(
            tab_ref.at[flip(deep, step)], tabbuf.at[step - 1], tab_send.at[step], tab_recv.at[step],
            device_id=deep_id(step), device_id_type=MESH)

    def tok_copy(step):
        return pltpu.make_async_remote_copy(
            tok_ref, tokbuf.at[step - 1], tok_send.at[step], tok_recv.at[step],
            device_id=deep_id(step), device_id_type=MESH)

    def part_copy(step, piece):
        return pltpu.make_async_remote_copy(
            psend.at[step - 1, piece], precv.at[step - 1, piece], p_send.at[step, piece], p_recv.at[step, piece],
            device_id=deep_id(step), device_id_type=MESH)

    for step in range(1, DEEP):
        tab_copy(step).start()

    def wait_bytes(ref, sem):
        pltpu.make_async_copy(ref, ref, sem).wait()

    def table(step):
        return tab_ref[deep] if step == 0 else tabbuf[step - 1]

    slots = lax.broadcasted_iota(jnp.int32, (pad, tokens), 0).astype(jnp.float32)

    def pack(step):
        slot = step % 2
        if step:
            tab_copy(step).wait_recv()
            tok_copy(step).wait_recv()
            if step + 1 < DEEP:
                tok_copy(step + 1).start()
        if step >= 2:
            wait_bytes(stage.at[slot, rest], x_send.at[step - 2])
        tab = table(step)
        pick = jnp.concatenate(
            [jnp.where(slots == tab[p:p + 1, :], 1.0, 0.0) for p in range(plane)], axis=0
        ).astype(jnp.bfloat16)
        source = tok_ref if step == 0 else tokbuf.at[step - 1]

        @pl.loop(0, width // 512)
        def _(i):
            cols = pl.ds(pl.multiple_of(i * 512, 512), 512)
            packed = jnp.dot(pick, source[:, cols], preferred_element_type=jnp.float32)
            stage[slot, :, cols] = packed.astype(jnp.bfloat16)

        @pl.loop(1, plane)
        def _(j):
            other = partner(plane - j)
            pltpu.make_async_remote_copy(
                stage.at[slot, slot_of(other)], xbuf.at[step, slot_of(me)], x_send.at[step], x_recv.at[step],
                device_id=peer_id(other), device_id_type=MESH).start()

        pltpu.make_async_copy(stage.at[slot, slot_of(me)], xbuf.at[step, slot_of(me)], x_recv.at[step]).start()

    def expert(step):
        wait_bytes(xbuf.at[step], x_recv.at[step])
        if step == 0:
            weights[0].wait()
            weights[1].wait()

        @pl.loop(0, ffw // 256)
        def _(i):
            cols = pl.ds(pl.multiple_of(i * 256, 256), 256)
            arrived = xbuf[step]
            gate = jnp.dot(arrived, wg[:, cols], preferred_element_type=jnp.float32)
            up = jnp.dot(arrived, wu[:, cols], preferred_element_type=jnp.float32)
            hid[:, cols] = (gate / (1.0 + jnp.exp(-gate)) * up).astype(jnp.bfloat16)

        if step == 0:
            weights[2].wait()

        @pl.loop(0, width // 512)
        def _(i):
            cols = pl.ds(pl.multiple_of(i * 512, 512), 512)
            given = jnp.dot(hid[...], wd[:, cols], preferred_element_type=jnp.float32)
            xbuf[step, :, cols] = given.astype(jnp.bfloat16)

    def give_back(step):
        for piece in range(PIECES):
            cols = pl.ds(piece * part, part)

            @pl.loop(1, plane)
            def _(j):
                other = partner(plane - j)
                pltpu.make_async_remote_copy(
                    xbuf.at[step, slot_of(other), cols], back.at[step, piece, slot_of(me)],
                    r_send.at[step, piece], r_recv.at[step, piece],
                    device_id=peer_id(other), device_id_type=MESH).start()

            pltpu.make_async_copy(
                xbuf.at[step, slot_of(me), cols], back.at[step, piece, slot_of(me)], r_recv.at[step, piece]).start()

    def combine(step):
        tab = table(step)
        share = jnp.concatenate(
            [jnp.where(slots == tab[p:p + 1, :], tab[plane + p:plane + p + 1, :], 0.0) for p in range(plane)],
            axis=0).T
        high = share.astype(jnp.bfloat16)
        low = (share - high.astype(jnp.float32)).astype(jnp.bfloat16)
        for piece in range(PIECES):
            wait_bytes(back.at[step, piece], r_recv.at[step, piece])
            held = near.at[step, piece] if resident else near
            if not resident:
                load = pltpu.make_async_copy(far.at[step, piece], near, l_sem)
                load.start()
                load.wait()

            @pl.loop(0, part // 512)
            def _(i):
                cols = pl.ds(pl.multiple_of(i * 512, 512), 512)
                given = held[:, cols]
                total = jnp.dot(high, given, preferred_element_type=jnp.float32)
                total = total + jnp.dot(low, given, preferred_element_type=jnp.float32)
                if step == 0:
                    own[piece, :, cols] = total
                else:
                    psend[step - 1, piece, :, cols] = total.astype(jnp.bfloat16)

            if step:
                part_copy(step, piece).start()

    tok_copy(1).start()
    pack(0)
    pack(1)
    expert(0)
    pack(2)
    expert(1)
    give_back(1)
    pack(3)
    expert(2)
    give_back(2)
    expert(3)
    give_back(3)
    give_back(0)
    combine(1)
    combine(2)
    combine(3)
    combine(0)
    for piece in range(PIECES):
        for step in range(1, DEEP):
            part_copy(step, piece).wait_recv()

        @pl.loop(0, part // 512)
        def _(i):
            cols = pl.ds(pl.multiple_of(i * 512, 512), 512)
            whole = pl.ds(pl.multiple_of(piece * part + i * 512, 512), 512)
            total = own[piece, :, cols]
            for step in range(1, DEEP):
                total = total + precv[step - 1, piece, :, cols].astype(jnp.float32)
            out_ref[:, whole] = total.astype(jnp.bfloat16)

    for step in range(1, DEEP):
        tab_copy(step).wait_send()
        tok_copy(step).wait_send()
        for piece in range(PIECES):
            part_copy(step, piece).wait_send()
    for step in range(DEEP):
        if step >= DEEP - 2:
            wait_bytes(stage.at[step % 2, rest], x_send.at[step])
        for piece in range(PIECES):
            wait_bytes(back.at[step, piece, rest], r_send.at[step, piece])


def grid_kernel(pad, tok_hbm, tab_ref, wg_hbm, wu_hbm, wd_hbm, out_ref,
                pair, tabs, stage, xbuf, hid, back, precv, zrecv, wg, wu, wd,
                wsem, tok_sem, own_sem, tab_send, tab_recv, za_send, za_recv, zb_send, zb_recv,
                f_send, f_recv, e_send, e_recv, x_send, x_recv, r_send, r_recv,
                p_send, p_recv, q_send, q_recv):
    tokens, width = out_ref.shape
    ffw = wg.shape[1]
    chunk = 2 * pad
    part = width // PIECES
    row = lax.axis_index("row")
    col = lax.axis_index("col")
    y, core = row // 2, row % 2
    z, x = col // 2, col % 2
    upper = z // 2
    middle = z * (3 - z) // 2
    inner = middle == 1
    f = y * (1 - core) + x * core
    l = x * (1 - core) + y * core
    order = (z, 1 - z + 4 * upper, 2 - upper, 3 - 3 * upper)
    onward = (None, 3 - z, 3 * upper, 3 * upper)

    def at(first, last, which, deep):
        return ((first * (1 - core) + last * core) * 2 + which, deep * 2 + last * (1 - core) + first * core)

    sibling = (y * 2 + 1 - core, col)
    twin = at(1 - f, l, core, z)
    mine = pl.ds(pl.multiple_of(f * tokens, tokens), tokens)
    other = pl.ds(pl.multiple_of((1 - f) * tokens, tokens), tokens)

    def chunk_at(slot):
        return pl.ds(pl.multiple_of(slot * chunk, 16), chunk)

    def send(src, dst, ssem, rsem, device):
        return pltpu.make_async_remote_copy(src, dst, ssem, rsem, device_id=device, device_id_type=MESH)

    def wait_bytes(ref, sem):
        pltpu.make_async_copy(ref, ref, sem).wait()

    barrier = pltpu.get_barrier_semaphore()

    def greet(device):
        pl.semaphore_signal(barrier, inc=1, device_id=device, device_id_type=MESH)

    greet(sibling)
    for which in range(2):
        greet((y * 2 + which, z * 2 + 1 - x))
        greet(((1 - y) * 2 + which, col))
    for j in range(1, DEEP):
        for g in range(2):
            greet(at((f + g) % 2, l, core, (z + j) % DEEP))

    weights = [pltpu.make_async_copy(src.at[0], dst, wsem.at[i])
               for i, (src, dst) in enumerate(((wg_hbm, wg), (wu_hbm, wu), (wd_hbm, wd)))]
    own_tok = pltpu.make_async_copy(tok_hbm, pair.at[z, mine], tok_sem.at[0])
    own_tab = pltpu.make_async_copy(tab_ref.at[z, f], tabs.at[z, f], tok_sem.at[1])
    own_tok.start()
    own_tab.start()
    pl.semaphore_wait(barrier, 5 + 2 * (DEEP - 1))

    early, late = pl.ds(0, CB), pl.ds(CB, width - CB)

    def early_copy():
        return send(tok_hbm.at[:, early], pair.at[z, mine, early], e_send, e_recv, twin)

    def first_copy(k):
        src = tok_hbm.at[:, late] if k == 0 else pair.at[order[k], mine, late]
        return send(src, pair.at[order[k], mine, late], f_send.at[k], f_recv.at[k], twin)

    def line_copy(block, index, target):
        src = tok_hbm if index < 2 else pair.at[block, mine]
        return send(src, pair.at[block, mine], za_send.at[index], za_recv.at[block], (row, target * 2 + x))

    def line_early(block, index, target):
        ref = pair.at[block, other, early]
        return send(ref, ref, zb_send.at[index], zb_recv.at[block], (row, target * 2 + x))

    if CB:
        early_copy().start()
    line_copy(z, 0, order[1]).start()

    @pl.when(inner)
    def _():
        line_copy(z, 1, onward[1]).start()

    for j in range(DEEP):
        for g in range(2):
            if j or g:
                who, deep = (f + g) % 2, (z + j) % DEEP
                send(tab_ref.at[deep, who], tabs.at[z, f], tab_send.at[j, g], tab_recv.at[z, f],
                     at(who, l, core, deep)).start()
    first_copy(0).start()
    for copy in weights:
        copy.start()
    if CB:
        early_copy().wait_recv()
        line_early(z, 0, order[1]).start()

        @pl.when(inner)
        def _():
            line_early(z, 1, onward[1]).start()

    def fetch(k):
        line_copy(order[k], 2, order[1]).wait_recv()
        first_copy(k).start()

        @pl.when(inner)
        def _():
            line_copy(order[k], 1 + k, onward[k]).start()

        if CB:
            line_early(order[k], 2, order[1]).wait_recv()

            @pl.when(inner)
            def _():
                line_early(order[k], 1 + k, onward[k]).start()

    places = lax.broadcasted_iota(jnp.int32, (chunk, tokens), 0).astype(jnp.float32)
    peers = [(l, core, None), (l, 1 - core, sibling),
             (1 - l, 0, at(f, 1 - l, 0, z)), (1 - l, 1, at(f, 1 - l, 1, z))]
    far = pl.ds(0, 3 * chunk)

    kept, primed = set(), set()

    def wait_kept(k):
        if k not in kept:
            kept.add(k)
            keep = chunk_at(l * 2 + core)
            wait_bytes(xbuf.at[k, keep], own_sem.at[k])

    def pack(k):
        slot = k % 2
        block = order[k]
        if k == 0:
            own_tok.wait()
            own_tab.wait()
            wait_bytes(tabs.at[block, 1 - f], tab_recv.at[block, 1 - f])
        else:
            wait_bytes(tabs.at[block, 0], tab_recv.at[block, 0])
            wait_bytes(tabs.at[block, 1], tab_recv.at[block, 1])
        first_copy(k).wait_recv()
        if k >= 2:
            wait_bytes(stage.at[slot, far], x_send.at[k - 2])
            wait_kept(k - 2)
        low_tab, high_tab = tabs[block, 0], tabs[block, 1]
        pick = jnp.concatenate(
            [jnp.concatenate([jnp.where(places == low_tab[j:j + 1, :], 1.0, 0.0),
                              jnp.where(places == high_tab[j:j + 1, :], 1.0, 0.0)], axis=1) for j in range(4)],
            axis=0).astype(jnp.bfloat16)
        for piece in range(PIECES):

            @pl.loop(0, part // 512)
            def _(i):
                cols = pl.ds(pl.multiple_of(piece * part + i * 512, 512), 512)
                packed = jnp.dot(pick, pair[block, :, cols], preferred_element_type=jnp.float32)
                stage[slot, :, cols] = packed.astype(jnp.bfloat16)

            cols = pl.ds(piece * part, part)
            for last, which, device in reversed(peers):
                src = stage.at[slot, chunk_at(last * 2 + which), cols]
                dst = xbuf.at[k, chunk_at(core * 2 + l), cols]
                if device is None:
                    pltpu.make_async_copy(src, dst, own_sem.at[k]).start()
                else:
                    send(src, dst, x_send.at[k], x_recv.at[k], device).start()

    holders = [(core, l, None), (1 - core, f, sibling),
               (0, 1 - x, (y * 2, z * 2 + 1 - x)), (1, 1 - y, ((1 - y) * 2 + 1, col))]

    def give_back(k, piece):
        cols = pl.ds(piece * part, part)
        for which, last, device in reversed(holders):
            place = x * (1 - which) + y * which
            src = xbuf.at[k, chunk_at(which * 2 + last), cols]
            dst = back.at[k, chunk_at(place * 2 + core), cols]
            if device is None:
                pltpu.make_async_copy(src, dst, r_recv.at[k, piece]).start()
            else:
                send(src, dst, r_send.at[k, piece], r_recv.at[k, piece], device).start()

    def expert(k, give):
        wait_bytes(xbuf.at[k, far], x_recv.at[k])
        wait_kept(k)
        if len(primed) == 0:
            weights[0].wait()
            weights[1].wait()

        @pl.loop(0, ffw // 256)
        def _(i):
            cols = pl.ds(pl.multiple_of(i * 256, 256), 256)
            arrived = xbuf[k]
            gate = jnp.dot(arrived, wg[:, cols], preferred_element_type=jnp.float32)
            up = jnp.dot(arrived, wu[:, cols], preferred_element_type=jnp.float32)
            hid[:, cols] = (gate / (1.0 + jnp.exp(-gate)) * up).astype(jnp.bfloat16)

        if len(primed) == 0:
            weights[2].wait()
        primed.add(k)
        for piece in range(PIECES):

            @pl.loop(0, part // 512)
            def _(i):
                cols = pl.ds(pl.multiple_of(piece * part + i * 512, 512), 512)
                given = jnp.dot(hid[...], wd[:, cols], preferred_element_type=jnp.float32)
                xbuf[k, :, cols] = given.astype(jnp.bfloat16)

            if give:
                give_back(k, piece)

    def share(k, half):
        tab = tabs[order[k], half]
        whole = jnp.concatenate(
            [jnp.where(places == tab[j:j + 1, :], tab[4 + j:5 + j, :], 0.0) for j in range(4)], axis=0).T
        high = whole.astype(jnp.bfloat16)
        low = (whole - high.astype(jnp.float32)).astype(jnp.bfloat16)
        return jnp.concatenate([high, low], axis=0)

    def mixed_of(both, k, cols):
        total = jnp.dot(both, back[k, :, cols], preferred_element_type=jnp.float32)
        return total[:tokens] + total[tokens:]

    def twin_copy(k, piece):
        cols = pl.ds(piece * part, part)
        return send(pair.at[order[k], other, cols], precv.at[k, :, cols],
                    p_send.at[k, piece], p_recv.at[k, piece], twin)

    def home_copy(k, piece):
        cols = pl.ds(piece * part, part)
        place = 0 if k == 1 else middle + (1 - middle) * k
        target = order[1] if k == 1 else middle * order[k] + (1 - middle) * order[1]
        return send(pair.at[order[k], mine, cols], zrecv.at[place, :, cols],
                    q_send.at[k, piece], q_recv.at[place, piece], (row, target * 2 + x))

    def combine_other(k):
        both = share(k, 1 - f)
        for piece in range(PIECES):
            wait_bytes(back.at[k, :, pl.ds(piece * part, part)], r_recv.at[k, piece])
            if CB and k and piece == 0:
                @pl.when(inner)
                def _():
                    line_early(order[k], 1 + k, onward[k]).wait_send()
            if CB and k == 0 and piece == 0:
                line_early(z, 0, order[1]).wait_send()

                @pl.when(inner)
                def _():
                    line_early(z, 1, onward[1]).wait_send()

            @pl.loop(0, part // 512)
            def _(i):
                cols = pl.ds(pl.multiple_of(piece * part + i * 512, 512), 512)
                pair[order[k], other, cols] = mixed_of(both, k, cols).astype(jnp.bfloat16)

            twin_copy(k, piece).start()

    def combine_own(k):
        both = share(k, f)
        if k:
            first_copy(k).wait_send()

            @pl.when(inner)
            def _():
                line_copy(order[k], 1 + k, onward[k]).wait_send()

        def add_up(piece, places, result):
            for place in places:
                wait_bytes(zrecv.at[place, :, pl.ds(piece * part, part)], q_recv.at[place, piece])

            @pl.loop(0, part // 512)
            def _(i):
                cols = pl.ds(pl.multiple_of(piece * part + i * 512, 512), 512)
                total = mixed_of(both, k, cols) + precv[k, :, cols].astype(jnp.float32)
                for place in places:
                    total = total + zrecv[place, :, cols].astype(jnp.float32)
                result[:, cols] = total.astype(jnp.bfloat16)

        for piece in range(PIECES):
            twin_copy(k, piece).wait_recv()
            if k == 0:
                add_up(piece, (0, 1), out_ref)
                continue
            result = pair.at[order[k], mine]
            if k == 1:
                add_up(piece, (), result)
            else:

                @pl.when(inner)
                def _():
                    add_up(piece, (k,), result)

                @pl.when(jnp.logical_not(inner))
                def _():
                    add_up(piece, (), result)

            home_copy(k, piece).start()

    pack(0)
    fetch(1)

    @pl.when(inner)
    def _():
        fetch(2)

    pack(1)

    @pl.when(inner)
    def _():
        fetch(3)


    @pl.when(jnp.logical_not(inner))
    def _():
        fetch(2)

    expert(1, True)

    @pl.when(jnp.logical_not(inner))
    def _():
        fetch(3)

    combine_other(1)
    pack(2)
    combine_own(1)
    expert(2, True)
    pack(3)
    combine_other(2)
    expert(3, True)
    combine_own(2)
    combine_other(3)
    expert(0, True)
    combine_own(3)
    combine_other(0)
    combine_own(0)

    if CB:
        early_copy().wait_send()
    first_copy(0).wait_send()
    line_copy(z, 0, order[1]).wait_send()

    @pl.when(inner)
    def _():
        line_copy(z, 1, onward[1]).wait_send()

    for j in range(DEEP):
        for g in range(2):
            if j or g:
                wait_bytes(tab_ref.at[j, g], tab_send.at[j, g])
    for k in (2, 3):
        wait_bytes(stage.at[k % 2, far], x_send.at[k])
    for k in range(DEEP):
        for piece in range(PIECES):
            wait_bytes(back.at[k, far, pl.ds(piece * part, part)], r_send.at[k, piece])
            twin_copy(k, piece).wait_send()
            if k:
                home_copy(k, piece).wait_send()


def grid_call(tokens, rank, gates, w_gate, w_up, w_down, pad):
    tok_count, width = tokens.shape
    ffw = w_gate.shape[2]
    row, col = lax.axis_index("row"), lax.axis_index("col")
    core = row % 2
    first = (row // 2) * (1 - core) + (col % 2) * core
    rank = jnp.where(rank < 0, rank, rank + (pad * first).astype(jnp.float32))
    both = jnp.stack([rank, gates]).reshape(2, tok_count, 2, 2, DEEP, 2)
    tab = jnp.where(core == 0, both.transpose(4, 2, 0, 5, 3, 1), both.transpose(4, 5, 0, 2, 3, 1))
    tab = tab.reshape(DEEP, 2, 8, tok_count)
    vmem = pl.BlockSpec(memory_space=pltpu.VMEM)
    anywhere = pl.BlockSpec(memory_space=pl.ANY)
    dma = pltpu.SemaphoreType.DMA
    return pl.pallas_call(
        functools.partial(grid_kernel, pad),
        out_shape=jax.ShapeDtypeStruct((tok_count, width), jnp.bfloat16),
        in_specs=[anywhere, vmem, anywhere, anywhere, anywhere],
        out_specs=vmem,
        scratch_shapes=[
            pltpu.VMEM((DEEP, 2 * tok_count, width), jnp.bfloat16),
            pltpu.VMEM((DEEP, 2, 8, tok_count), jnp.float32),
            pltpu.VMEM((2, 8 * pad, width), jnp.bfloat16),
            pltpu.VMEM((DEEP, 8 * pad, width), jnp.bfloat16),
            pltpu.VMEM((8 * pad, ffw), jnp.bfloat16),
            pltpu.VMEM((DEEP, 8 * pad, width), jnp.bfloat16),
            pltpu.VMEM((DEEP, tok_count, width), jnp.bfloat16),
            pltpu.VMEM((DEEP, tok_count, width), jnp.bfloat16),
            pltpu.VMEM(w_gate.shape[1:], jnp.bfloat16),
            pltpu.VMEM(w_up.shape[1:], jnp.bfloat16),
            pltpu.VMEM(w_down.shape[1:], jnp.bfloat16),
            dma((3,)), dma((2,)), dma((DEEP,)), dma((DEEP, 2)), dma((DEEP, 2)), dma((5,)), dma((DEEP,)), dma((5,)), dma((DEEP,)),
            dma((DEEP,)), dma((DEEP,)), dma, dma, dma((DEEP,)), dma((DEEP,)),
            dma((DEEP, PIECES)), dma((DEEP, PIECES)), dma((DEEP, PIECES)), dma((DEEP, PIECES)),
            dma((DEEP, PIECES)), dma((DEEP, PIECES)),
        ],
        compiler_params=pltpu.CompilerParams(
            collective_id=1, has_side_effects=True, vmem_limit_bytes=63 * 1024 * 1024),
    )(tokens, tab, w_gate, w_up, w_down)


def per_device(tokens, expert_ids, router_weight, w_gate, w_up, w_down):
    tok_count, width = tokens.shape
    top_count = expert_ids.shape[1]
    experts = router_weight.shape[1]
    ffw = w_gate.shape[2]
    rows_axis = lax.axis_size("row")
    cols_axis = lax.axis_size("col")
    side = cols_axis // DEEP
    plane = rows_axis * side
    cap = tok_count * top_count * 5 // (4 * experts)
    pad = -(-cap // 8) * 8

    logits = jnp.dot(tokens, router_weight, preferred_element_type=jnp.float32)
    named = jnp.any(expert_ids[:, :, None] == jnp.arange(experts, dtype=jnp.int32)[None, None, :], axis=1)
    top = jnp.max(jnp.where(named, logits, -jnp.inf), axis=1, keepdims=True)
    scores = jnp.where(named, jnp.exp(jnp.where(named, logits - top, 0.0)), 0.0)
    gates = scores / jnp.sum(scores, axis=1, keepdims=True)
    before = jnp.tril(jnp.ones((tok_count, tok_count), jnp.bfloat16), -1)
    rank = jnp.dot(before, named.astype(jnp.bfloat16), preferred_element_type=jnp.float32)
    rank = jnp.where(named, rank, -1.0)
    if (rows_axis, cols_axis) == (4, 2 * DEEP):
        return grid_call(tokens, rank, gates, w_gate, w_up, w_down, pad)
    both = jnp.stack([rank, gates]).reshape(2, tok_count, rows_axis, DEEP, side)
    tab = both.transpose(3, 0, 2, 4, 1).reshape(DEEP, 2 * plane, tok_count)

    vmem = pl.BlockSpec(memory_space=pltpu.VMEM)
    anywhere = pl.BlockSpec(memory_space=pl.ANY)
    dma = pltpu.SemaphoreType.DMA
    back_dims = (DEEP, PIECES, plane * pad, width // PIECES)
    resident = 4 * DEEP * plane * pad * width <= 24 * 1024 * 1024
    mixed = jax.ShapeDtypeStruct((tok_count, width), jnp.bfloat16)
    given = pl.pallas_call(
        functools.partial(moe_kernel, (rows_axis, side, pad, resident)),
        out_shape=(mixed,) if resident else (mixed, jax.ShapeDtypeStruct(back_dims, jnp.bfloat16)),
        in_specs=[vmem, vmem, anywhere, anywhere, anywhere],
        out_specs=(vmem,) if resident else (vmem, anywhere),
        scratch_shapes=[
            pltpu.VMEM((DEEP - 1, tok_count, width), jnp.bfloat16),
            pltpu.VMEM((DEEP - 1, 2 * plane, tok_count), jnp.float32),
            pltpu.VMEM((2, plane * pad, width), jnp.bfloat16),
            pltpu.VMEM((DEEP, plane * pad, width), jnp.bfloat16),
            pltpu.VMEM((plane * pad, ffw), jnp.bfloat16),
            pltpu.VMEM(back_dims if resident else back_dims[2:], jnp.bfloat16),
            pltpu.VMEM((DEEP - 1, PIECES, tok_count, width // PIECES), jnp.bfloat16),
            pltpu.VMEM((DEEP - 1, PIECES, tok_count, width // PIECES), jnp.bfloat16),
            pltpu.VMEM((PIECES, tok_count, width // PIECES), jnp.float32),
            pltpu.VMEM(w_gate.shape[1:], jnp.bfloat16),
            pltpu.VMEM(w_up.shape[1:], jnp.bfloat16),
            pltpu.VMEM(w_down.shape[1:], jnp.bfloat16),
            dma((3,)), dma((DEEP,)), dma((DEEP,)), dma((DEEP,)), dma((DEEP,)), dma((DEEP,)), dma((DEEP,)),
            dma((DEEP, PIECES)), dma((DEEP, PIECES)), dma((DEEP, PIECES)), dma((DEEP, PIECES)), dma,
        ],
        compiler_params=pltpu.CompilerParams(
            collective_id=0, has_side_effects=True, vmem_limit_bytes=63 * 1024 * 1024),
    )(tokens, tab, w_gate, w_up, w_down)
    return given[0]


def solution(mesh):
    placed = (
        P(("row", "col"), None),
        P(("row", "col"), None),
        P(),
        P(("row", "col"), None, None),
        P(("row", "col"), None, None),
        P(("row", "col"), None, None),
    )
    return jax.shard_map(
        per_device, mesh=mesh, in_specs=placed, out_specs=P(("row", "col"), None), check_vma=False
    )
```

```python
import functools

import jax
import jax.numpy as jnp
from jax import lax
from jax.experimental import pallas as pl
from jax.experimental.pallas import tpu as pltpu
from jax.sharding import PartitionSpec as P

MESH = pl.DeviceIdType.MESH
DEEP = 4
PIECES = 4
CB = 2048


def flip(index, step):
    bit = step & 1
    if bit:
        index = index + 1 - 2 * (index % 2)
    if step & 2:
        index = index + 2 - 4 * ((index // 2) % 2)
    return index


def moe_kernel(dims, tok_ref, tab_ref, wg_hbm, wu_hbm, wd_hbm, out_ref, *refs):
    rows_axis, side, pad, resident = dims
    far = None if resident else refs[0]
    (tokbuf, tabbuf, stage, xbuf, hid, near, psend, precv, own, wg, wu, wd,
     wsem, tok_send, tok_recv, tab_send, tab_recv, x_send, x_recv,
     r_send, r_recv, p_send, p_recv, l_sem) = refs if resident else refs[1:]
    back = near if resident else far
    plane = rows_axis * side
    tokens, width = tok_ref.shape
    ffw = wg.shape[1]
    part = width // PIECES
    row = lax.axis_index("row")
    col = lax.axis_index("col")
    deep = col // side
    across = col % side
    me = row * side + across
    rest = pl.ds(0, (plane - 1) * pad)

    def slot_of(other):
        return pl.ds(pl.multiple_of(other * pad, 8), pad)

    def peer_id(other):
        return (other // side, deep * side + other % side)

    def partner(j):
        if plane & (plane - 1):
            return (me + j) % plane
        return sum(bit * ((me // bit + j // bit) % 2) for bit in (1 << i for i in range(plane.bit_length() - 1)))

    def deep_id(step):
        return (row, flip(deep, step) * side + across)

    barrier = pltpu.get_barrier_semaphore()

    @pl.loop(1, plane)
    def _(j):
        pl.semaphore_signal(barrier, inc=1, device_id=peer_id((me + j) % plane), device_id_type=MESH)

    for step in range(1, DEEP):
        pl.semaphore_signal(barrier, inc=1, device_id=deep_id(step), device_id_type=MESH)

    weights = [pltpu.make_async_copy(src.at[0], dst, wsem.at[i])
               for i, (src, dst) in enumerate(((wg_hbm, wg), (wu_hbm, wu), (wd_hbm, wd)))]
    for copy in weights:
        copy.start()
    pl.semaphore_wait(barrier, plane - 1 + DEEP - 1)

    def tab_copy(step):
        return pltpu.make_async_remote_copy(
            tab_ref.at[flip(deep, step)], tabbuf.at[step - 1], tab_send.at[step], tab_recv.at[step],
            device_id=deep_id(step), device_id_type=MESH)

    def tok_copy(step):
        return pltpu.make_async_remote_copy(
            tok_ref, tokbuf.at[step - 1], tok_send.at[step], tok_recv.at[step],
            device_id=deep_id(step), device_id_type=MESH)

    def part_copy(step, piece):
        return pltpu.make_async_remote_copy(
            psend.at[step - 1, piece], precv.at[step - 1, piece], p_send.at[step, piece], p_recv.at[step, piece],
            device_id=deep_id(step), device_id_type=MESH)

    for step in range(1, DEEP):
        tab_copy(step).start()

    def wait_bytes(ref, sem):
        pltpu.make_async_copy(ref, ref, sem).wait()

    def table(step):
        return tab_ref[deep] if step == 0 else tabbuf[step - 1]

    slots = lax.broadcasted_iota(jnp.int32, (pad, tokens), 0).astype(jnp.float32)

    def pack(step):
        slot = step % 2
        if step:
            tab_copy(step).wait_recv()
            tok_copy(step).wait_recv()
            if step + 1 < DEEP:
                tok_copy(step + 1).start()
        if step >= 2:
            wait_bytes(stage.at[slot, rest], x_send.at[step - 2])
        tab = table(step)
        pick = jnp.concatenate(
            [jnp.where(slots == tab[p:p + 1, :], 1.0, 0.0) for p in range(plane)], axis=0
        ).astype(jnp.bfloat16)
        source = tok_ref if step == 0 else tokbuf.at[step - 1]

        @pl.loop(0, width // 512)
        def _(i):
            cols = pl.ds(pl.multiple_of(i * 512, 512), 512)
            packed = jnp.dot(pick, source[:, cols], preferred_element_type=jnp.float32)
            stage[slot, :, cols] = packed.astype(jnp.bfloat16)

        @pl.loop(1, plane)
        def _(j):
            other = partner(plane - j)
            pltpu.make_async_remote_copy(
                stage.at[slot, slot_of(other)], xbuf.at[step, slot_of(me)], x_send.at[step], x_recv.at[step],
                device_id=peer_id(other), device_id_type=MESH).start()

        pltpu.make_async_copy(stage.at[slot, slot_of(me)], xbuf.at[step, slot_of(me)], x_recv.at[step]).start()

    def expert(step):
        wait_bytes(xbuf.at[step], x_recv.at[step])
        if step == 0:
            weights[0].wait()
            weights[1].wait()

        @pl.loop(0, ffw // 256)
        def _(i):
            cols = pl.ds(pl.multiple_of(i * 256, 256), 256)
            arrived = xbuf[step]
            gate = jnp.dot(arrived, wg[:, cols], preferred_element_type=jnp.float32)
            up = jnp.dot(arrived, wu[:, cols], preferred_element_type=jnp.float32)
            hid[:, cols] = (gate / (1.0 + jnp.exp(-gate)) * up).astype(jnp.bfloat16)

        if step == 0:
            weights[2].wait()

        @pl.loop(0, width // 512)
        def _(i):
            cols = pl.ds(pl.multiple_of(i * 512, 512), 512)
            given = jnp.dot(hid[...], wd[:, cols], preferred_element_type=jnp.float32)
            xbuf[step, :, cols] = given.astype(jnp.bfloat16)

    def give_back(step):
        for piece in range(PIECES):
            cols = pl.ds(piece * part, part)

            @pl.loop(1, plane)
            def _(j):
                other = partner(plane - j)
                pltpu.make_async_remote_copy(
                    xbuf.at[step, slot_of(other), cols], back.at[step, piece, slot_of(me)],
                    r_send.at[step, piece], r_recv.at[step, piece],
                    device_id=peer_id(other), device_id_type=MESH).start()

            pltpu.make_async_copy(
                xbuf.at[step, slot_of(me), cols], back.at[step, piece, slot_of(me)], r_recv.at[step, piece]).start()

    def combine(step):
        tab = table(step)
        share = jnp.concatenate(
            [jnp.where(slots == tab[p:p + 1, :], tab[plane + p:plane + p + 1, :], 0.0) for p in range(plane)],
            axis=0).T
        high = share.astype(jnp.bfloat16)
        low = (share - high.astype(jnp.float32)).astype(jnp.bfloat16)
        for piece in range(PIECES):
            wait_bytes(back.at[step, piece], r_recv.at[step, piece])
            held = near.at[step, piece] if resident else near
            if not resident:
                load = pltpu.make_async_copy(far.at[step, piece], near, l_sem)
                load.start()
                load.wait()

            @pl.loop(0, part // 512)
            def _(i):
                cols = pl.ds(pl.multiple_of(i * 512, 512), 512)
                given = held[:, cols]
                total = jnp.dot(high, given, preferred_element_type=jnp.float32)
                total = total + jnp.dot(low, given, preferred_element_type=jnp.float32)
                if step == 0:
                    own[piece, :, cols] = total
                else:
                    psend[step - 1, piece, :, cols] = total.astype(jnp.bfloat16)

            if step:
                part_copy(step, piece).start()

    tok_copy(1).start()
    pack(0)
    pack(1)
    expert(0)
    pack(2)
    expert(1)
    give_back(1)
    pack(3)
    expert(2)
    give_back(2)
    expert(3)
    give_back(3)
    give_back(0)
    combine(1)
    combine(2)
    combine(3)
    combine(0)
    for piece in range(PIECES):
        for step in range(1, DEEP):
            part_copy(step, piece).wait_recv()

        @pl.loop(0, part // 512)
        def _(i):
            cols = pl.ds(pl.multiple_of(i * 512, 512), 512)
            whole = pl.ds(pl.multiple_of(piece * part + i * 512, 512), 512)
            total = own[piece, :, cols]
            for step in range(1, DEEP):
                total = total + precv[step - 1, piece, :, cols].astype(jnp.float32)
            out_ref[:, whole] = total.astype(jnp.bfloat16)

    for step in range(1, DEEP):
        tab_copy(step).wait_send()
        tok_copy(step).wait_send()
        for piece in range(PIECES):
            part_copy(step, piece).wait_send()
    for step in range(DEEP):
        if step >= DEEP - 2:
            wait_bytes(stage.at[step % 2, rest], x_send.at[step])
        for piece in range(PIECES):
            wait_bytes(back.at[step, piece, rest], r_send.at[step, piece])


def grid_kernel(pad, tok_hbm, tab_ref, wg_hbm, wu_hbm, wd_hbm, out_ref,
                pair, tabs, stage, xbuf, hid, back, precv, zrecv, wg, wu, wd,
                wsem, tok_sem, own_sem, tab_send, tab_recv, za_send, za_recv, zb_send, zb_recv,
                f_send, f_recv, e_send, e_recv, x_send, x_recv, r_send, r_recv,
                p_send, p_recv, q_send, q_recv):
    tokens, width = out_ref.shape
    ffw = wg.shape[1]
    chunk = 2 * pad
    part = width // PIECES
    row = lax.axis_index("row")
    col = lax.axis_index("col")
    y, core = row // 2, row % 2
    z, x = col // 2, col % 2
    upper = z // 2
    middle = z * (3 - z) // 2
    inner = middle == 1
    f = y * (1 - core) + x * core
    l = x * (1 - core) + y * core
    order = (z, 1 - z + 4 * upper, 2 - upper, 3 - 3 * upper)
    onward = (None, 3 - z, 3 * upper, 3 * upper)

    def at(first, last, which, deep):
        return ((first * (1 - core) + last * core) * 2 + which, deep * 2 + last * (1 - core) + first * core)

    sibling = (y * 2 + 1 - core, col)
    twin = at(1 - f, l, core, z)
    mine = pl.ds(pl.multiple_of(f * tokens, tokens), tokens)
    other = pl.ds(pl.multiple_of((1 - f) * tokens, tokens), tokens)

    def chunk_at(slot):
        return pl.ds(pl.multiple_of(slot * chunk, 16), chunk)

    def send(src, dst, ssem, rsem, device):
        return pltpu.make_async_remote_copy(src, dst, ssem, rsem, device_id=device, device_id_type=MESH)

    def wait_bytes(ref, sem):
        pltpu.make_async_copy(ref, ref, sem).wait()

    barrier = pltpu.get_barrier_semaphore()

    def greet(device):
        pl.semaphore_signal(barrier, inc=1, device_id=device, device_id_type=MESH)

    greet(sibling)
    for which in range(2):
        greet((y * 2 + which, z * 2 + 1 - x))
        greet(((1 - y) * 2 + which, col))
    for j in range(1, DEEP):
        for g in range(2):
            greet(at((f + g) % 2, l, core, (z + j) % DEEP))

    weights = [pltpu.make_async_copy(src.at[0], dst, wsem.at[i])
               for i, (src, dst) in enumerate(((wg_hbm, wg), (wu_hbm, wu), (wd_hbm, wd)))]
    own_tok = pltpu.make_async_copy(tok_hbm, pair.at[z, mine], tok_sem.at[0])
    own_tab = pltpu.make_async_copy(tab_ref.at[z, f], tabs.at[z, f], tok_sem.at[1])
    own_tok.start()
    own_tab.start()
    pl.semaphore_wait(barrier, 5 + 2 * (DEEP - 1))

    early, late = pl.ds(0, CB), pl.ds(CB, width - CB)

    def early_copy():
        return send(tok_hbm.at[:, early], pair.at[z, mine, early], e_send, e_recv, twin)

    def first_copy(k):
        src = tok_hbm.at[:, late] if k == 0 else pair.at[order[k], mine, late]
        return send(src, pair.at[order[k], mine, late], f_send.at[k], f_recv.at[k], twin)

    def line_copy(block, index, target):
        src = tok_hbm if index < 2 else pair.at[block, mine]
        return send(src, pair.at[block, mine], za_send.at[index], za_recv.at[block], (row, target * 2 + x))

    def line_early(block, index, target):
        ref = pair.at[block, other, early]
        return send(ref, ref, zb_send.at[index], zb_recv.at[block], (row, target * 2 + x))

    if CB:
        early_copy().start()
    line_copy(z, 0, order[1]).start()

    @pl.when(inner)
    def _():
        line_copy(z, 1, onward[1]).start()

    for j in range(DEEP):
        for g in range(2):
            if j or g:
                who, deep = (f + g) % 2, (z + j) % DEEP
                send(tab_ref.at[deep, who], tabs.at[z, f], tab_send.at[j, g], tab_recv.at[z, f],
                     at(who, l, core, deep)).start()
    first_copy(0).start()
    for copy in weights:
        copy.start()
    if CB:
        early_copy().wait_recv()
        line_early(z, 0, order[1]).start()

        @pl.when(inner)
        def _():
            line_early(z, 1, onward[1]).start()

    def fetch(k):
        line_copy(order[k], 2, order[1]).wait_recv()
        first_copy(k).start()

        @pl.when(inner)
        def _():
            line_copy(order[k], 1 + k, onward[k]).start()

        if CB:
            line_early(order[k], 2, order[1]).wait_recv()

            @pl.when(inner)
            def _():
                line_early(order[k], 1 + k, onward[k]).start()

    places = lax.broadcasted_iota(jnp.int32, (chunk, tokens), 0).astype(jnp.float32)
    peers = [(l, core, None), (l, 1 - core, sibling),
             (1 - l, 0, at(f, 1 - l, 0, z)), (1 - l, 1, at(f, 1 - l, 1, z))]
    far = pl.ds(0, 3 * chunk)

    kept, primed = set(), set()

    def wait_kept(k):
        if k not in kept:
            kept.add(k)
            keep = chunk_at(l * 2 + core)
            wait_bytes(xbuf.at[k, keep], own_sem.at[k])

    def pack(k):
        slot = k % 2
        block = order[k]
        if k == 0:
            own_tok.wait()
            own_tab.wait()
            wait_bytes(tabs.at[block, 1 - f], tab_recv.at[block, 1 - f])
        else:
            wait_bytes(tabs.at[block, 0], tab_recv.at[block, 0])
            wait_bytes(tabs.at[block, 1], tab_recv.at[block, 1])
        first_copy(k).wait_recv()
        if k >= 2:
            wait_bytes(stage.at[slot, far], x_send.at[k - 2])
            wait_kept(k - 2)
        low_tab, high_tab = tabs[block, 0], tabs[block, 1]
        pick = jnp.concatenate(
            [jnp.concatenate([jnp.where(places == low_tab[j:j + 1, :], 1.0, 0.0),
                              jnp.where(places == high_tab[j:j + 1, :], 1.0, 0.0)], axis=1) for j in range(4)],
            axis=0).astype(jnp.bfloat16)
        for piece in range(PIECES):

            @pl.loop(0, part // 512)
            def _(i):
                cols = pl.ds(pl.multiple_of(piece * part + i * 512, 512), 512)
                packed = jnp.dot(pick, pair[block, :, cols], preferred_element_type=jnp.float32)
                stage[slot, :, cols] = packed.astype(jnp.bfloat16)

            cols = pl.ds(piece * part, part)
            for last, which, device in reversed(peers):
                src = stage.at[slot, chunk_at(last * 2 + which), cols]
                dst = xbuf.at[k, chunk_at(core * 2 + l), cols]
                if device is None:
                    pltpu.make_async_copy(src, dst, own_sem.at[k]).start()
                else:
                    send(src, dst, x_send.at[k], x_recv.at[k], device).start()

    holders = [(core, l, None), (1 - core, f, sibling),
               (0, 1 - x, (y * 2, z * 2 + 1 - x)), (1, 1 - y, ((1 - y) * 2 + 1, col))]

    def give_back(k, piece):
        cols = pl.ds(piece * part, part)
        for which, last, device in reversed(holders):
            place = x * (1 - which) + y * which
            src = xbuf.at[k, chunk_at(which * 2 + last), cols]
            dst = back.at[k, chunk_at(place * 2 + core), cols]
            if device is None:
                pltpu.make_async_copy(src, dst, r_recv.at[k, piece]).start()
            else:
                send(src, dst, r_send.at[k, piece], r_recv.at[k, piece], device).start()

    def expert(k, give):
        wait_bytes(xbuf.at[k, far], x_recv.at[k])
        wait_kept(k)
        if len(primed) == 0:
            weights[0].wait()
            weights[1].wait()

        @pl.loop(0, ffw // 256)
        def _(i):
            cols = pl.ds(pl.multiple_of(i * 256, 256), 256)
            arrived = xbuf[k]
            gate = jnp.dot(arrived, wg[:, cols], preferred_element_type=jnp.float32)
            up = jnp.dot(arrived, wu[:, cols], preferred_element_type=jnp.float32)
            hid[:, cols] = (gate / (1.0 + jnp.exp(-gate)) * up).astype(jnp.bfloat16)

        if len(primed) == 0:
            weights[2].wait()
        primed.add(k)
        for piece in range(PIECES):

            @pl.loop(0, part // 512)
            def _(i):
                cols = pl.ds(pl.multiple_of(piece * part + i * 512, 512), 512)
                given = jnp.dot(hid[...], wd[:, cols], preferred_element_type=jnp.float32)
                xbuf[k, :, cols] = given.astype(jnp.bfloat16)

            if give:
                give_back(k, piece)

    def share(k, half):
        tab = tabs[order[k], half]
        whole = jnp.concatenate(
            [jnp.where(places == tab[j:j + 1, :], tab[4 + j:5 + j, :], 0.0) for j in range(4)], axis=0).T
        high = whole.astype(jnp.bfloat16)
        low = (whole - high.astype(jnp.float32)).astype(jnp.bfloat16)
        return jnp.concatenate([high, low], axis=0)

    def mixed_of(both, k, cols):
        total = jnp.dot(both, back[k, :, cols], preferred_element_type=jnp.float32)
        return total[:tokens] + total[tokens:]

    def twin_copy(k, piece):
        cols = pl.ds(piece * part, part)
        return send(pair.at[order[k], other, cols], precv.at[k, :, cols],
                    p_send.at[k, piece], p_recv.at[k, piece], twin)

    def home_copy(k, piece):
        cols = pl.ds(piece * part, part)
        place = 0 if k == 1 else middle + (1 - middle) * k
        target = order[1] if k == 1 else middle * order[k] + (1 - middle) * order[1]
        return send(pair.at[order[k], mine, cols], zrecv.at[place, :, cols],
                    q_send.at[k, piece], q_recv.at[place, piece], (row, target * 2 + x))

    def combine_other(k):
        both = share(k, 1 - f)
        for piece in range(PIECES):
            wait_bytes(back.at[k, :, pl.ds(piece * part, part)], r_recv.at[k, piece])
            if CB and k and piece == 0:
                @pl.when(inner)
                def _():
                    line_early(order[k], 1 + k, onward[k]).wait_send()
            if CB and k == 0 and piece == 0:
                line_early(z, 0, order[1]).wait_send()

                @pl.when(inner)
                def _():
                    line_early(z, 1, onward[1]).wait_send()

            @pl.loop(0, part // 512)
            def _(i):
                cols = pl.ds(pl.multiple_of(piece * part + i * 512, 512), 512)
                pair[order[k], other, cols] = mixed_of(both, k, cols).astype(jnp.bfloat16)

            twin_copy(k, piece).start()

    def combine_own(k):
        both = share(k, f)
        if k:
            first_copy(k).wait_send()

            @pl.when(inner)
            def _():
                line_copy(order[k], 1 + k, onward[k]).wait_send()

        def add_up(piece, places, result):
            for place in places:
                wait_bytes(zrecv.at[place, :, pl.ds(piece * part, part)], q_recv.at[place, piece])

            @pl.loop(0, part // 512)
            def _(i):
                cols = pl.ds(pl.multiple_of(piece * part + i * 512, 512), 512)
                total = mixed_of(both, k, cols) + precv[k, :, cols].astype(jnp.float32)
                for place in places:
                    total = total + zrecv[place, :, cols].astype(jnp.float32)
                result[:, cols] = total.astype(jnp.bfloat16)

        for piece in range(PIECES):
            twin_copy(k, piece).wait_recv()
            if k == 0:
                add_up(piece, (0, 1), out_ref)
                continue
            result = pair.at[order[k], mine]
            if k == 1:
                add_up(piece, (), result)
            else:

                @pl.when(inner)
                def _():
                    add_up(piece, (k,), result)

                @pl.when(jnp.logical_not(inner))
                def _():
                    add_up(piece, (), result)

            home_copy(k, piece).start()

    pack(0)
    fetch(1)

    @pl.when(inner)
    def _():
        fetch(2)

    pack(1)
    expert(1, True)

    @pl.when(inner)
    def _():
        fetch(3)


    @pl.when(jnp.logical_not(inner))
    def _():
        fetch(2)

    combine_other(1)
    expert(0, False)
    pack(2)

    @pl.when(jnp.logical_not(inner))
    def _():
        fetch(3)

    pack(3)
    expert(2, False)
    combine_own(1)
    for piece in range(PIECES):
        give_back(2, piece)
    expert(3, False)
    combine_other(2)
    for piece in range(PIECES):
        give_back(3, piece)
    combine_own(2)
    combine_other(3)
    for piece in range(PIECES):
        give_back(0, piece)
    combine_own(3)
    combine_other(0)
    combine_own(0)

    if CB:
        early_copy().wait_send()
    first_copy(0).wait_send()
    line_copy(z, 0, order[1]).wait_send()

    @pl.when(inner)
    def _():
        line_copy(z, 1, onward[1]).wait_send()

    for j in range(DEEP):
        for g in range(2):
            if j or g:
                wait_bytes(tab_ref.at[j, g], tab_send.at[j, g])
    for k in (2, 3):
        wait_bytes(stage.at[k % 2, far], x_send.at[k])
    for k in range(DEEP):
        for piece in range(PIECES):
            wait_bytes(back.at[k, far, pl.ds(piece * part, part)], r_send.at[k, piece])
            twin_copy(k, piece).wait_send()
            if k:
                home_copy(k, piece).wait_send()


def grid_call(tokens, rank, gates, w_gate, w_up, w_down, pad):
    tok_count, width = tokens.shape
    ffw = w_gate.shape[2]
    row, col = lax.axis_index("row"), lax.axis_index("col")
    core = row % 2
    first = (row // 2) * (1 - core) + (col % 2) * core
    rank = jnp.where(rank < 0, rank, rank + (pad * first).astype(jnp.float32))
    both = jnp.stack([rank, gates]).reshape(2, tok_count, 2, 2, DEEP, 2)
    tab = jnp.where(core == 0, both.transpose(4, 2, 0, 5, 3, 1), both.transpose(4, 5, 0, 2, 3, 1))
    tab = tab.reshape(DEEP, 2, 8, tok_count)
    vmem = pl.BlockSpec(memory_space=pltpu.VMEM)
    anywhere = pl.BlockSpec(memory_space=pl.ANY)
    dma = pltpu.SemaphoreType.DMA
    return pl.pallas_call(
        functools.partial(grid_kernel, pad),
        out_shape=jax.ShapeDtypeStruct((tok_count, width), jnp.bfloat16),
        in_specs=[anywhere, vmem, anywhere, anywhere, anywhere],
        out_specs=vmem,
        scratch_shapes=[
            pltpu.VMEM((DEEP, 2 * tok_count, width), jnp.bfloat16),
            pltpu.VMEM((DEEP, 2, 8, tok_count), jnp.float32),
            pltpu.VMEM((2, 8 * pad, width), jnp.bfloat16),
            pltpu.VMEM((DEEP, 8 * pad, width), jnp.bfloat16),
            pltpu.VMEM((8 * pad, ffw), jnp.bfloat16),
            pltpu.VMEM((DEEP, 8 * pad, width), jnp.bfloat16),
            pltpu.VMEM((DEEP, tok_count, width), jnp.bfloat16),
            pltpu.VMEM((DEEP, tok_count, width), jnp.bfloat16),
            pltpu.VMEM(w_gate.shape[1:], jnp.bfloat16),
            pltpu.VMEM(w_up.shape[1:], jnp.bfloat16),
            pltpu.VMEM(w_down.shape[1:], jnp.bfloat16),
            dma((3,)), dma((2,)), dma((DEEP,)), dma((DEEP, 2)), dma((DEEP, 2)), dma((5,)), dma((DEEP,)), dma((5,)), dma((DEEP,)),
            dma((DEEP,)), dma((DEEP,)), dma, dma, dma((DEEP,)), dma((DEEP,)),
            dma((DEEP, PIECES)), dma((DEEP, PIECES)), dma((DEEP, PIECES)), dma((DEEP, PIECES)),
            dma((DEEP, PIECES)), dma((DEEP, PIECES)),
        ],
        compiler_params=pltpu.CompilerParams(
            collective_id=1, has_side_effects=True, vmem_limit_bytes=63 * 1024 * 1024),
    )(tokens, tab, w_gate, w_up, w_down)


def per_device(tokens, expert_ids, router_weight, w_gate, w_up, w_down):
    tok_count, width = tokens.shape
    top_count = expert_ids.shape[1]
    experts = router_weight.shape[1]
    ffw = w_gate.shape[2]
    rows_axis = lax.axis_size("row")
    cols_axis = lax.axis_size("col")
    side = cols_axis // DEEP
    plane = rows_axis * side
    cap = tok_count * top_count * 5 // (4 * experts)
    pad = -(-cap // 8) * 8

    logits = jnp.dot(tokens, router_weight, preferred_element_type=jnp.float32)
    named = jnp.any(expert_ids[:, :, None] == jnp.arange(experts, dtype=jnp.int32)[None, None, :], axis=1)
    top = jnp.max(jnp.where(named, logits, -jnp.inf), axis=1, keepdims=True)
    scores = jnp.where(named, jnp.exp(jnp.where(named, logits - top, 0.0)), 0.0)
    gates = scores / jnp.sum(scores, axis=1, keepdims=True)
    before = jnp.tril(jnp.ones((tok_count, tok_count), jnp.bfloat16), -1)
    rank = jnp.dot(before, named.astype(jnp.bfloat16), preferred_element_type=jnp.float32)
    rank = jnp.where(named, rank, -1.0)
    if (rows_axis, cols_axis) == (4, 2 * DEEP):
        return grid_call(tokens, rank, gates, w_gate, w_up, w_down, pad)
    both = jnp.stack([rank, gates]).reshape(2, tok_count, rows_axis, DEEP, side)
    tab = both.transpose(3, 0, 2, 4, 1).reshape(DEEP, 2 * plane, tok_count)

    vmem = pl.BlockSpec(memory_space=pltpu.VMEM)
    anywhere = pl.BlockSpec(memory_space=pl.ANY)
    dma = pltpu.SemaphoreType.DMA
    back_dims = (DEEP, PIECES, plane * pad, width // PIECES)
    resident = 4 * DEEP * plane * pad * width <= 24 * 1024 * 1024
    mixed = jax.ShapeDtypeStruct((tok_count, width), jnp.bfloat16)
    given = pl.pallas_call(
        functools.partial(moe_kernel, (rows_axis, side, pad, resident)),
        out_shape=(mixed,) if resident else (mixed, jax.ShapeDtypeStruct(back_dims, jnp.bfloat16)),
        in_specs=[vmem, vmem, anywhere, anywhere, anywhere],
        out_specs=(vmem,) if resident else (vmem, anywhere),
        scratch_shapes=[
            pltpu.VMEM((DEEP - 1, tok_count, width), jnp.bfloat16),
            pltpu.VMEM((DEEP - 1, 2 * plane, tok_count), jnp.float32),
            pltpu.VMEM((2, plane * pad, width), jnp.bfloat16),
            pltpu.VMEM((DEEP, plane * pad, width), jnp.bfloat16),
            pltpu.VMEM((plane * pad, ffw), jnp.bfloat16),
            pltpu.VMEM(back_dims if resident else back_dims[2:], jnp.bfloat16),
            pltpu.VMEM((DEEP - 1, PIECES, tok_count, width // PIECES), jnp.bfloat16),
            pltpu.VMEM((DEEP - 1, PIECES, tok_count, width // PIECES), jnp.bfloat16),
            pltpu.VMEM((PIECES, tok_count, width // PIECES), jnp.float32),
            pltpu.VMEM(w_gate.shape[1:], jnp.bfloat16),
            pltpu.VMEM(w_up.shape[1:], jnp.bfloat16),
            pltpu.VMEM(w_down.shape[1:], jnp.bfloat16),
            dma((3,)), dma((DEEP,)), dma((DEEP,)), dma((DEEP,)), dma((DEEP,)), dma((DEEP,)), dma((DEEP,)),
            dma((DEEP, PIECES)), dma((DEEP, PIECES)), dma((DEEP, PIECES)), dma((DEEP, PIECES)), dma,
        ],
        compiler_params=pltpu.CompilerParams(
            collective_id=0, has_side_effects=True, vmem_limit_bytes=63 * 1024 * 1024),
    )(tokens, tab, w_gate, w_up, w_down)
    return given[0]


def solution(mesh):
    placed = (
        P(("row", "col"), None),
        P(("row", "col"), None),
        P(),
        P(("row", "col"), None, None),
        P(("row", "col"), None, None),
        P(("row", "col"), None, None),
    )
    return jax.shard_map(
        per_device, mesh=mesh, in_specs=placed, out_specs=P(("row", "col"), None), check_vma=False
    )
```

```python
import functools

import jax
import jax.numpy as jnp
from jax import lax
from jax.experimental import pallas as pl
from jax.experimental.pallas import tpu as pltpu
from jax.sharding import PartitionSpec as P

MESH = pl.DeviceIdType.MESH
DEEP = 4
PIECES = 4
CB = 2048
UP = 256
DOWN = 512
TILE = 512


def flip(index, step):
    bit = step & 1
    if bit:
        index = index + 1 - 2 * (index % 2)
    if step & 2:
        index = index + 2 - 4 * ((index // 2) % 2)
    return index


def moe_kernel(dims, tok_ref, tab_ref, wg_hbm, wu_hbm, wd_hbm, out_ref, *refs):
    rows_axis, side, pad, resident = dims
    far = None if resident else refs[0]
    (tokbuf, tabbuf, stage, xbuf, hid, near, psend, precv, own, wg, wu, wd,
     wsem, tok_send, tok_recv, tab_send, tab_recv, x_send, x_recv,
     r_send, r_recv, p_send, p_recv, l_sem) = refs if resident else refs[1:]
    back = near if resident else far
    plane = rows_axis * side
    tokens, width = tok_ref.shape
    ffw = wg.shape[1]
    part = width // PIECES
    row = lax.axis_index("row")
    col = lax.axis_index("col")
    deep = col // side
    across = col % side
    me = row * side + across
    rest = pl.ds(0, (plane - 1) * pad)

    def slot_of(other):
        return pl.ds(pl.multiple_of(other * pad, 8), pad)

    def peer_id(other):
        return (other // side, deep * side + other % side)

    def partner(j):
        if plane & (plane - 1):
            return (me + j) % plane
        return sum(bit * ((me // bit + j // bit) % 2) for bit in (1 << i for i in range(plane.bit_length() - 1)))

    def deep_id(step):
        return (row, flip(deep, step) * side + across)

    barrier = pltpu.get_barrier_semaphore()

    @pl.loop(1, plane)
    def _(j):
        pl.semaphore_signal(barrier, inc=1, device_id=peer_id((me + j) % plane), device_id_type=MESH)

    for step in range(1, DEEP):
        pl.semaphore_signal(barrier, inc=1, device_id=deep_id(step), device_id_type=MESH)

    weights = [pltpu.make_async_copy(src.at[0], dst, wsem.at[i])
               for i, (src, dst) in enumerate(((wg_hbm, wg), (wu_hbm, wu), (wd_hbm, wd)))]
    for copy in weights:
        copy.start()
    pl.semaphore_wait(barrier, plane - 1 + DEEP - 1)

    def tab_copy(step):
        return pltpu.make_async_remote_copy(
            tab_ref.at[flip(deep, step)], tabbuf.at[step - 1], tab_send.at[step], tab_recv.at[step],
            device_id=deep_id(step), device_id_type=MESH)

    def tok_copy(step):
        return pltpu.make_async_remote_copy(
            tok_ref, tokbuf.at[step - 1], tok_send.at[step], tok_recv.at[step],
            device_id=deep_id(step), device_id_type=MESH)

    def part_copy(step, piece):
        return pltpu.make_async_remote_copy(
            psend.at[step - 1, piece], precv.at[step - 1, piece], p_send.at[step, piece], p_recv.at[step, piece],
            device_id=deep_id(step), device_id_type=MESH)

    for step in range(1, DEEP):
        tab_copy(step).start()

    def wait_bytes(ref, sem):
        pltpu.make_async_copy(ref, ref, sem).wait()

    def table(step):
        return tab_ref[deep] if step == 0 else tabbuf[step - 1]

    slots = lax.broadcasted_iota(jnp.int32, (pad, tokens), 0).astype(jnp.float32)

    def pack(step):
        slot = step % 2
        if step:
            tab_copy(step).wait_recv()
            tok_copy(step).wait_recv()
            if step + 1 < DEEP:
                tok_copy(step + 1).start()
        if step >= 2:
            wait_bytes(stage.at[slot, rest], x_send.at[step - 2])
        tab = table(step)
        pick = jnp.concatenate(
            [jnp.where(slots == tab[p:p + 1, :], 1.0, 0.0) for p in range(plane)], axis=0
        ).astype(jnp.bfloat16)
        source = tok_ref if step == 0 else tokbuf.at[step - 1]

        @pl.loop(0, width // 512)
        def _(i):
            cols = pl.ds(pl.multiple_of(i * 512, 512), 512)
            packed = jnp.dot(pick, source[:, cols], preferred_element_type=jnp.float32)
            stage[slot, :, cols] = packed.astype(jnp.bfloat16)

        @pl.loop(1, plane)
        def _(j):
            other = partner(plane - j)
            pltpu.make_async_remote_copy(
                stage.at[slot, slot_of(other)], xbuf.at[step, slot_of(me)], x_send.at[step], x_recv.at[step],
                device_id=peer_id(other), device_id_type=MESH).start()

        pltpu.make_async_copy(stage.at[slot, slot_of(me)], xbuf.at[step, slot_of(me)], x_recv.at[step]).start()

    def expert(step):
        wait_bytes(xbuf.at[step], x_recv.at[step])
        if step == 0:
            weights[0].wait()
            weights[1].wait()

        @pl.loop(0, ffw // 256)
        def _(i):
            cols = pl.ds(pl.multiple_of(i * 256, 256), 256)
            arrived = xbuf[step]
            gate = jnp.dot(arrived, wg[:, cols], preferred_element_type=jnp.float32)
            up = jnp.dot(arrived, wu[:, cols], preferred_element_type=jnp.float32)
            hid[:, cols] = (gate / (1.0 + jnp.exp(-gate)) * up).astype(jnp.bfloat16)

        if step == 0:
            weights[2].wait()

        @pl.loop(0, width // 512)
        def _(i):
            cols = pl.ds(pl.multiple_of(i * 512, 512), 512)
            given = jnp.dot(hid[...], wd[:, cols], preferred_element_type=jnp.float32)
            xbuf[step, :, cols] = given.astype(jnp.bfloat16)

    def give_back(step):
        for piece in range(PIECES):
            cols = pl.ds(piece * part, part)

            @pl.loop(1, plane)
            def _(j):
                other = partner(plane - j)
                pltpu.make_async_remote_copy(
                    xbuf.at[step, slot_of(other), cols], back.at[step, piece, slot_of(me)],
                    r_send.at[step, piece], r_recv.at[step, piece],
                    device_id=peer_id(other), device_id_type=MESH).start()

            pltpu.make_async_copy(
                xbuf.at[step, slot_of(me), cols], back.at[step, piece, slot_of(me)], r_recv.at[step, piece]).start()

    def combine(step):
        tab = table(step)
        share = jnp.concatenate(
            [jnp.where(slots == tab[p:p + 1, :], tab[plane + p:plane + p + 1, :], 0.0) for p in range(plane)],
            axis=0).T
        high = share.astype(jnp.bfloat16)
        low = (share - high.astype(jnp.float32)).astype(jnp.bfloat16)
        for piece in range(PIECES):
            wait_bytes(back.at[step, piece], r_recv.at[step, piece])
            held = near.at[step, piece] if resident else near
            if not resident:
                load = pltpu.make_async_copy(far.at[step, piece], near, l_sem)
                load.start()
                load.wait()

            @pl.loop(0, part // 512)
            def _(i):
                cols = pl.ds(pl.multiple_of(i * 512, 512), 512)
                given = held[:, cols]
                total = jnp.dot(high, given, preferred_element_type=jnp.float32)
                total = total + jnp.dot(low, given, preferred_element_type=jnp.float32)
                if step == 0:
                    own[piece, :, cols] = total
                else:
                    psend[step - 1, piece, :, cols] = total.astype(jnp.bfloat16)

            if step:
                part_copy(step, piece).start()

    tok_copy(1).start()
    pack(0)
    pack(1)
    expert(0)
    pack(2)
    expert(1)
    give_back(1)
    pack(3)
    expert(2)
    give_back(2)
    expert(3)
    give_back(3)
    give_back(0)
    combine(1)
    combine(2)
    combine(3)
    combine(0)
    for piece in range(PIECES):
        for step in range(1, DEEP):
            part_copy(step, piece).wait_recv()

        @pl.loop(0, part // 512)
        def _(i):
            cols = pl.ds(pl.multiple_of(i * 512, 512), 512)
            whole = pl.ds(pl.multiple_of(piece * part + i * 512, 512), 512)
            total = own[piece, :, cols]
            for step in range(1, DEEP):
                total = total + precv[step - 1, piece, :, cols].astype(jnp.float32)
            out_ref[:, whole] = total.astype(jnp.bfloat16)

    for step in range(1, DEEP):
        tab_copy(step).wait_send()
        tok_copy(step).wait_send()
        for piece in range(PIECES):
            part_copy(step, piece).wait_send()
    for step in range(DEEP):
        if step >= DEEP - 2:
            wait_bytes(stage.at[step % 2, rest], x_send.at[step])
        for piece in range(PIECES):
            wait_bytes(back.at[step, piece, rest], r_send.at[step, piece])


def grid_kernel(pad, tok_hbm, ids_hbm, router_hbm, wg_hbm, wu_hbm, wd_hbm, out_hbm,
                ids_ref, router_ref, tab_ref, pair, tabs, stage, xbuf, hid, back, precv, zrecv, wg, wu, wd,
                wsem, tok_sem, own_sem, tab_send, tab_recv, za_send, za_recv, zb_send, zb_recv,
                f_send, f_recv, e_send, e_recv, x_send, x_recv, r_send, r_recv,
                p_send, p_recv, q_send, q_recv, o_sem):
    tokens, width = tok_hbm.shape
    ffw = wg.shape[1]
    chunk = 2 * pad
    part = width // PIECES
    row = lax.axis_index("row")
    col = lax.axis_index("col")
    y, core = row // 2, row % 2
    z, x = col // 2, col % 2
    upper = z // 2
    middle = z * (3 - z) // 2
    inner = middle == 1
    f = y * (1 - core) + x * core
    l = x * (1 - core) + y * core
    order = (z, 1 - z + 4 * upper, 2 - upper, 3 - 3 * upper)
    onward = (None, 3 - z, 3 * upper, 3 * upper)

    def at(first, last, which, deep):
        return ((first * (1 - core) + last * core) * 2 + which, deep * 2 + last * (1 - core) + first * core)

    sibling = (y * 2 + 1 - core, col)
    twin = at(1 - f, l, core, z)
    mine = pl.ds(pl.multiple_of(f * tokens, tokens), tokens)
    other = pl.ds(pl.multiple_of((1 - f) * tokens, tokens), tokens)

    def chunk_at(slot):
        return pl.ds(pl.multiple_of(slot * chunk, 16), chunk)

    def send(src, dst, ssem, rsem, device):
        return pltpu.make_async_remote_copy(src, dst, ssem, rsem, device_id=device, device_id_type=MESH)

    def wait_bytes(ref, sem):
        pltpu.make_async_copy(ref, ref, sem).wait()

    barrier = pltpu.get_barrier_semaphore()

    def greet(device):
        pl.semaphore_signal(barrier, inc=1, device_id=device, device_id_type=MESH)

    greet(sibling)
    for which in range(2):
        greet((y * 2 + which, z * 2 + 1 - x))
        greet(((1 - y) * 2 + which, col))
    for j in range(1, DEEP):
        for g in range(2):
            greet(at((f + g) % 2, l, core, (z + j) % DEEP))

    weights = [pltpu.make_async_copy(src.at[0], dst, wsem.at[i])
               for i, (src, dst) in enumerate(((wg_hbm, wg), (wu_hbm, wu), (wd_hbm, wd)))]
    own_tok = pltpu.make_async_copy(tok_hbm, pair.at[z, mine], tok_sem.at[0])
    own_ids = pltpu.make_async_copy(ids_hbm, ids_ref, tok_sem.at[1])
    own_router = pltpu.make_async_copy(router_hbm, router_ref, tok_sem.at[2])
    for copy in (own_tok, own_ids, own_router):
        copy.start()
    pl.semaphore_wait(barrier, 5 + 2 * (DEEP - 1))

    early, late = pl.ds(0, CB), pl.ds(CB, width - CB)

    def early_copy():
        return send(tok_hbm.at[:, early], pair.at[z, mine, early], e_send, e_recv, twin)

    def first_copy(k):
        src = tok_hbm.at[:, late] if k == 0 else pair.at[order[k], mine, late]
        return send(src, pair.at[order[k], mine, late], f_send.at[k], f_recv.at[k], twin)

    def line_copy(block, index, target):
        src = tok_hbm if index < 2 else pair.at[block, mine]
        return send(src, pair.at[block, mine], za_send.at[index], za_recv.at[block], (row, target * 2 + x))

    def line_early(block, index, target):
        ref = pair.at[block, other, early]
        return send(ref, ref, zb_send.at[index], zb_recv.at[block], (row, target * 2 + x))

    if CB:
        early_copy().start()
    line_copy(z, 0, order[1]).start()

    @pl.when(inner)
    def _():
        line_copy(z, 1, onward[1]).start()

    first_copy(0).start()
    for copy in weights:
        copy.start()
    if CB:
        early_copy().wait_recv()
        line_early(z, 0, order[1]).start()

        @pl.when(inner)
        def _():
            line_early(z, 1, onward[1]).start()

    own_tok.wait()
    own_ids.wait()
    own_router.wait()
    experts = router_ref.shape[0]
    logits = lax.dot_general(router_ref[...], pair[z, mine, :], (((1,), (1,)), ((), ())),
                             preferred_element_type=jnp.float32)
    number = lax.broadcasted_iota(jnp.int32, (experts, tokens), 0)
    count = sum(jnp.where(number == ids_ref[k:k + 1, :], 1.0, 0.0) for k in range(ids_ref.shape[0]))
    named = count > 0.5
    top = jnp.max(jnp.where(named, logits, -jnp.inf), axis=0, keepdims=True)
    scores = jnp.where(named, jnp.exp(jnp.where(named, logits - top, 0.0)), 0.0)
    gates = scores / jnp.sum(scores, axis=0, keepdims=True)
    before = jnp.where(lax.broadcasted_iota(jnp.int32, (tokens, tokens), 0)
                       < lax.broadcasted_iota(jnp.int32, (tokens, tokens), 1), 1.0, 0.0).astype(jnp.bfloat16)
    rank = jnp.dot(count.astype(jnp.bfloat16), before, preferred_element_type=jnp.float32)
    rank = jnp.where(named, rank + (pad * f).astype(jnp.float32), -1.0)
    for deep in range(DEEP):
        for who in range(2):
            straight = [((who * 2 + j % 2) * DEEP + deep) * 2 + j // 2 for j in range(4)]
            turned = [((j // 2 * 2 + j % 2) * DEEP + deep) * 2 + who for j in range(4)]
            tab_ref[deep, who] = jnp.where(
                core == 0,
                jnp.concatenate([v[e:e + 1] for v in (rank, gates) for e in straight], axis=0),
                jnp.concatenate([v[e:e + 1] for v in (rank, gates) for e in turned], axis=0))

    for j in range(DEEP):
        for g in range(2):
            if j or g:
                who, deep = (f + g) % 2, (z + j) % DEEP
                send(tab_ref.at[deep, who], tabs.at[z, f], tab_send.at[j, g], tab_recv.at[z, f],
                     at(who, l, core, deep)).start()
    tabs[z, f] = tab_ref[z, f]

    def fetch(k):
        line_copy(order[k], 2, order[1]).wait_recv()
        first_copy(k).start()

        @pl.when(inner)
        def _():
            line_copy(order[k], 1 + k, onward[k]).start()

        if CB:
            line_early(order[k], 2, order[1]).wait_recv()

            @pl.when(inner)
            def _():
                line_early(order[k], 1 + k, onward[k]).start()

    places = lax.broadcasted_iota(jnp.int32, (chunk, tokens), 0).astype(jnp.float32)
    peers = [(l, core, None), (l, 1 - core, sibling),
             (1 - l, 0, at(f, 1 - l, 0, z)), (1 - l, 1, at(f, 1 - l, 1, z))]
    far = pl.ds(0, 3 * chunk)

    kept, primed = set(), set()

    def wait_kept(k):
        if k not in kept:
            kept.add(k)
            keep = chunk_at(l * 2 + core)
            wait_bytes(xbuf.at[k, keep], own_sem.at[k])

    def pack(k):
        slot = k % 2
        block = order[k]
        if k == 0:
            wait_bytes(tabs.at[block, 1 - f], tab_recv.at[block, 1 - f])
        else:
            wait_bytes(tabs.at[block, 0], tab_recv.at[block, 0])
            wait_bytes(tabs.at[block, 1], tab_recv.at[block, 1])
        first_copy(k).wait_recv()
        if k >= 2:
            wait_bytes(stage.at[slot, far], x_send.at[k - 2])
            wait_kept(k - 2)
        low_tab, high_tab = tabs[block, 0], tabs[block, 1]
        pick = jnp.concatenate(
            [jnp.concatenate([jnp.where(places == low_tab[j:j + 1, :], 1.0, 0.0),
                              jnp.where(places == high_tab[j:j + 1, :], 1.0, 0.0)], axis=1) for j in range(4)],
            axis=0).astype(jnp.bfloat16)
        for piece in range(PIECES):

            @pl.loop(0, part // TILE)
            def _(i):
                cols = pl.ds(pl.multiple_of(piece * part + i * TILE, TILE), TILE)
                packed = jnp.dot(pick, pair[block, :, cols], preferred_element_type=jnp.float32)
                stage[slot, :, cols] = packed.astype(jnp.bfloat16)

            cols = pl.ds(piece * part, part)
            for last, which, device in reversed(peers):
                src = stage.at[slot, chunk_at(last * 2 + which), cols]
                dst = xbuf.at[k, chunk_at(core * 2 + l), cols]
                if device is None:
                    pltpu.make_async_copy(src, dst, own_sem.at[k]).start()
                else:
                    send(src, dst, x_send.at[k], x_recv.at[k], device).start()

    holders = [(core, l, None), (1 - core, f, sibling),
               (0, 1 - x, (y * 2, z * 2 + 1 - x)), (1, 1 - y, ((1 - y) * 2 + 1, col))]

    def give_back(k, piece):
        cols = pl.ds(piece * part, part)
        for which, last, device in reversed(holders):
            place = x * (1 - which) + y * which
            src = xbuf.at[k, chunk_at(which * 2 + last), cols]
            dst = back.at[k, chunk_at(place * 2 + core), cols]
            if device is None:
                pltpu.make_async_copy(src, dst, r_recv.at[k, piece]).start()
            else:
                send(src, dst, r_send.at[k, piece], r_recv.at[k, piece], device).start()

    def expert_in(k):
        wait_bytes(xbuf.at[k, far], x_recv.at[k])
        wait_kept(k)
        if len(primed) == 0:
            weights[0].wait()
            weights[1].wait()

        @pl.loop(0, ffw // UP)
        def _(i):
            cols = pl.ds(pl.multiple_of(i * UP, UP), UP)
            arrived = xbuf[k]
            gate = jnp.dot(arrived, wg[:, cols], preferred_element_type=jnp.float32)
            up = jnp.dot(arrived, wu[:, cols], preferred_element_type=jnp.float32)
            hid[:, cols] = (gate / (1.0 + jnp.exp(-gate)) * up).astype(jnp.bfloat16)

    def expert_out(k, give):
        if len(primed) == 0:
            weights[2].wait()
        primed.add(k)
        for piece in range(PIECES):

            @pl.loop(0, part // DOWN)
            def _(i):
                cols = pl.ds(pl.multiple_of(piece * part + i * DOWN, DOWN), DOWN)
                given = jnp.dot(hid[...], wd[:, cols], preferred_element_type=jnp.float32)
                xbuf[k, :, cols] = given.astype(jnp.bfloat16)

            if give:
                give_back(k, piece)

    def share(k, half):
        tab = tabs[order[k], half]
        whole = jnp.concatenate(
            [jnp.where(places == tab[j:j + 1, :], tab[4 + j:5 + j, :], 0.0) for j in range(4)], axis=0).T
        high = whole.astype(jnp.bfloat16)
        low = (whole - high.astype(jnp.float32)).astype(jnp.bfloat16)
        return jnp.concatenate([high, low], axis=0)

    def mixed_of(both, k, cols):
        total = jnp.dot(both, back[k, :, cols], preferred_element_type=jnp.float32)
        return total[:tokens] + total[tokens:]

    def twin_copy(k, piece):
        cols = pl.ds(piece * part, part)
        return send(pair.at[order[k], other, cols], precv.at[k, :, cols],
                    p_send.at[k, piece], p_recv.at[k, piece], twin)

    def home_copy(k, piece):
        cols = pl.ds(piece * part, part)
        place = 0 if k == 1 else middle + (1 - middle) * k
        target = order[1] if k == 1 else middle * order[k] + (1 - middle) * order[1]
        return send(pair.at[order[k], mine, cols], zrecv.at[place, :, cols],
                    q_send.at[k, piece], q_recv.at[place, piece], (row, target * 2 + x))

    def combine_other(k):
        both = share(k, 1 - f)
        for piece in range(PIECES):
            wait_bytes(back.at[k, :, pl.ds(piece * part, part)], r_recv.at[k, piece])
            if CB and k and piece == 0:
                @pl.when(inner)
                def _():
                    line_early(order[k], 1 + k, onward[k]).wait_send()
            if CB and k == 0 and piece == 0:
                line_early(z, 0, order[1]).wait_send()

                @pl.when(inner)
                def _():
                    line_early(z, 1, onward[1]).wait_send()

            @pl.loop(0, part // TILE)
            def _(i):
                cols = pl.ds(pl.multiple_of(piece * part + i * TILE, TILE), TILE)
                pair[order[k], other, cols] = mixed_of(both, k, cols).astype(jnp.bfloat16)

            twin_copy(k, piece).start()

    def out_copy(piece):
        cols = pl.ds(piece * part, part)
        return pltpu.make_async_copy(pair.at[z, mine, cols], out_hbm.at[:, cols], o_sem.at[piece])

    def combine_own(k):
        both = share(k, f)
        if k:
            first_copy(k).wait_send()

            @pl.when(inner)
            def _():
                line_copy(order[k], 1 + k, onward[k]).wait_send()

        def add_up(piece, places, result):
            for place in places:
                wait_bytes(zrecv.at[place, :, pl.ds(piece * part, part)], q_recv.at[place, piece])

            @pl.loop(0, part // TILE)
            def _(i):
                cols = pl.ds(pl.multiple_of(piece * part + i * TILE, TILE), TILE)
                total = mixed_of(both, k, cols) + precv[k, :, cols].astype(jnp.float32)
                for place in places:
                    total = total + zrecv[place, :, cols].astype(jnp.float32)
                result[:, cols] = total.astype(jnp.bfloat16)

        for piece in range(PIECES):
            twin_copy(k, piece).wait_recv()
            result = pair.at[order[k], mine]
            if k == 0:
                add_up(piece, (0, 1), result)
                out_copy(piece).start()
                continue
            if k == 1:
                add_up(piece, (), result)
            else:

                @pl.when(inner)
                def _():
                    add_up(piece, (k,), result)

                @pl.when(jnp.logical_not(inner))
                def _():
                    add_up(piece, (), result)

            home_copy(k, piece).start()

    pack(0)
    fetch(1)

    @pl.when(inner)
    def _():
        fetch(2)

    pack(1)
    expert_in(1)
    expert_out(1, True)

    @pl.when(inner)
    def _():
        fetch(3)


    @pl.when(jnp.logical_not(inner))
    def _():
        fetch(2)

    combine_other(1)
    expert_in(0)
    expert_out(0, False)
    pack(2)

    @pl.when(jnp.logical_not(inner))
    def _():
        fetch(3)

    pack(3)
    expert_in(2)
    expert_out(2, False)
    combine_own(1)
    for piece in range(PIECES):
        give_back(2, piece)
    expert_in(3)
    expert_out(3, False)
    combine_other(2)
    for piece in range(PIECES):
        give_back(3, piece)
    combine_own(2)
    combine_other(3)
    for piece in range(PIECES):
        give_back(0, piece)
    combine_own(3)
    combine_other(0)
    combine_own(0)

    if CB:
        early_copy().wait_send()
    first_copy(0).wait_send()
    line_copy(z, 0, order[1]).wait_send()

    @pl.when(inner)
    def _():
        line_copy(z, 1, onward[1]).wait_send()

    for j in range(DEEP):
        for g in range(2):
            if j or g:
                wait_bytes(tab_ref.at[j, g], tab_send.at[j, g])
    for k in (2, 3):
        wait_bytes(stage.at[k % 2, far], x_send.at[k])
    for k in range(DEEP):
        for piece in range(PIECES):
            if k == 0:
                out_copy(piece).wait()
            wait_bytes(back.at[k, far, pl.ds(piece * part, part)], r_send.at[k, piece])
            twin_copy(k, piece).wait_send()
            if k:
                home_copy(k, piece).wait_send()


def grid_call(tokens, expert_ids, router_weight, w_gate, w_up, w_down):
    tok_count, width = tokens.shape
    top_count = expert_ids.shape[1]
    experts = router_weight.shape[1]
    ffw = w_gate.shape[2]
    pad = tok_count * top_count * 5 // (4 * experts)
    anywhere = pl.BlockSpec(memory_space=pl.ANY)
    dma = pltpu.SemaphoreType.DMA
    return pl.pallas_call(
        functools.partial(grid_kernel, pad),
        out_shape=jax.ShapeDtypeStruct((tok_count, width), jnp.bfloat16),
        in_specs=[anywhere] * 6,
        out_specs=anywhere,
        scratch_shapes=[
            pltpu.VMEM((top_count, tok_count), jnp.int32),
            pltpu.VMEM((experts, width), jnp.bfloat16),
            pltpu.VMEM((DEEP, 2, 8, tok_count), jnp.float32),
            pltpu.VMEM((DEEP, 2 * tok_count, width), jnp.bfloat16),
            pltpu.VMEM((DEEP, 2, 8, tok_count), jnp.float32),
            pltpu.VMEM((2, 8 * pad, width), jnp.bfloat16),
            pltpu.VMEM((DEEP, 8 * pad, width), jnp.bfloat16),
            pltpu.VMEM((8 * pad, ffw), jnp.bfloat16),
            pltpu.VMEM((DEEP, 8 * pad, width), jnp.bfloat16),
            pltpu.VMEM((DEEP, tok_count, width), jnp.bfloat16),
            pltpu.VMEM((DEEP, tok_count, width), jnp.bfloat16),
            pltpu.VMEM(w_gate.shape[1:], jnp.bfloat16),
            pltpu.VMEM(w_up.shape[1:], jnp.bfloat16),
            pltpu.VMEM(w_down.shape[1:], jnp.bfloat16),
            dma((3,)), dma((3,)), dma((DEEP,)), dma((DEEP, 2)), dma((DEEP, 2)), dma((5,)), dma((DEEP,)), dma((5,)), dma((DEEP,)),
            dma((DEEP,)), dma((DEEP,)), dma, dma, dma((DEEP,)), dma((DEEP,)),
            dma((DEEP, PIECES)), dma((DEEP, PIECES)), dma((DEEP, PIECES)), dma((DEEP, PIECES)),
            dma((DEEP, PIECES)), dma((DEEP, PIECES)), dma((PIECES,)),
        ],
        compiler_params=pltpu.CompilerParams(
            collective_id=1, has_side_effects=True, vmem_limit_bytes=63 * 1024 * 1024),
    )(tokens, expert_ids.T, router_weight.T, w_gate, w_up, w_down)


def per_device(tokens, expert_ids, router_weight, w_gate, w_up, w_down):
    tok_count, width = tokens.shape
    top_count = expert_ids.shape[1]
    experts = router_weight.shape[1]
    ffw = w_gate.shape[2]
    rows_axis = lax.axis_size("row")
    cols_axis = lax.axis_size("col")
    side = cols_axis // DEEP
    plane = rows_axis * side
    cap = tok_count * top_count * 5 // (4 * experts)
    pad = -(-cap // 8) * 8

    if (rows_axis, cols_axis) == (4, 2 * DEEP):
        return grid_call(tokens, expert_ids, router_weight, w_gate, w_up, w_down)

    logits = jnp.dot(tokens, router_weight, preferred_element_type=jnp.float32)
    named = jnp.any(expert_ids[:, :, None] == jnp.arange(experts, dtype=jnp.int32)[None, None, :], axis=1)
    top = jnp.max(jnp.where(named, logits, -jnp.inf), axis=1, keepdims=True)
    scores = jnp.where(named, jnp.exp(jnp.where(named, logits - top, 0.0)), 0.0)
    gates = scores / jnp.sum(scores, axis=1, keepdims=True)
    before = jnp.tril(jnp.ones((tok_count, tok_count), jnp.bfloat16), -1)
    rank = jnp.dot(before, named.astype(jnp.bfloat16), preferred_element_type=jnp.float32)
    rank = jnp.where(named, rank, -1.0)
    both = jnp.stack([rank, gates]).reshape(2, tok_count, rows_axis, DEEP, side)
    tab = both.transpose(3, 0, 2, 4, 1).reshape(DEEP, 2 * plane, tok_count)

    vmem = pl.BlockSpec(memory_space=pltpu.VMEM)
    anywhere = pl.BlockSpec(memory_space=pl.ANY)
    dma = pltpu.SemaphoreType.DMA
    back_dims = (DEEP, PIECES, plane * pad, width // PIECES)
    resident = 4 * DEEP * plane * pad * width <= 24 * 1024 * 1024
    mixed = jax.ShapeDtypeStruct((tok_count, width), jnp.bfloat16)
    given = pl.pallas_call(
        functools.partial(moe_kernel, (rows_axis, side, pad, resident)),
        out_shape=(mixed,) if resident else (mixed, jax.ShapeDtypeStruct(back_dims, jnp.bfloat16)),
        in_specs=[vmem, vmem, anywhere, anywhere, anywhere],
        out_specs=(vmem,) if resident else (vmem, anywhere),
        scratch_shapes=[
            pltpu.VMEM((DEEP - 1, tok_count, width), jnp.bfloat16),
            pltpu.VMEM((DEEP - 1, 2 * plane, tok_count), jnp.float32),
            pltpu.VMEM((2, plane * pad, width), jnp.bfloat16),
            pltpu.VMEM((DEEP, plane * pad, width), jnp.bfloat16),
            pltpu.VMEM((plane * pad, ffw), jnp.bfloat16),
            pltpu.VMEM(back_dims if resident else back_dims[2:], jnp.bfloat16),
            pltpu.VMEM((DEEP - 1, PIECES, tok_count, width // PIECES), jnp.bfloat16),
            pltpu.VMEM((DEEP - 1, PIECES, tok_count, width // PIECES), jnp.bfloat16),
            pltpu.VMEM((PIECES, tok_count, width // PIECES), jnp.float32),
            pltpu.VMEM(w_gate.shape[1:], jnp.bfloat16),
            pltpu.VMEM(w_up.shape[1:], jnp.bfloat16),
            pltpu.VMEM(w_down.shape[1:], jnp.bfloat16),
            dma((3,)), dma((DEEP,)), dma((DEEP,)), dma((DEEP,)), dma((DEEP,)), dma((DEEP,)), dma((DEEP,)),
            dma((DEEP, PIECES)), dma((DEEP, PIECES)), dma((DEEP, PIECES)), dma((DEEP, PIECES)), dma,
        ],
        compiler_params=pltpu.CompilerParams(
            collective_id=0, has_side_effects=True, vmem_limit_bytes=63 * 1024 * 1024),
    )(tokens, tab, w_gate, w_up, w_down)
    return given[0]


def solution(mesh):
    placed = (
        P(("row", "col"), None),
        P(("row", "col"), None),
        P(),
        P(("row", "col"), None, None),
        P(("row", "col"), None, None),
        P(("row", "col"), None, None),
    )
    return jax.shard_map(
        per_device, mesh=mesh, in_specs=placed, out_specs=P(("row", "col"), None), check_vma=False
    )
```

```python
import functools

import jax
import jax.numpy as jnp
from jax import lax
from jax.experimental import pallas as pl
from jax.experimental.pallas import tpu as pltpu
from jax.sharding import PartitionSpec as P

MESH = pl.DeviceIdType.MESH
DEEP = 4
PIECES = 4
CB = 2048
UP = 256
DOWN = 512
TILE = 512
EARLY = range(CB * PIECES // 4096)
LATE = range(CB * PIECES // 4096, PIECES)


def flip(index, step):
    bit = step & 1
    if bit:
        index = index + 1 - 2 * (index % 2)
    if step & 2:
        index = index + 2 - 4 * ((index // 2) % 2)
    return index


def moe_kernel(dims, tok_ref, tab_ref, wg_hbm, wu_hbm, wd_hbm, out_ref, *refs):
    rows_axis, side, pad, resident = dims
    far = None if resident else refs[0]
    (tokbuf, tabbuf, stage, xbuf, hid, near, psend, precv, own, wg, wu, wd,
     wsem, tok_send, tok_recv, tab_send, tab_recv, x_send, x_recv,
     r_send, r_recv, p_send, p_recv, l_sem) = refs if resident else refs[1:]
    back = near if resident else far
    plane = rows_axis * side
    tokens, width = tok_ref.shape
    ffw = wg.shape[1]
    part = width // PIECES
    row = lax.axis_index("row")
    col = lax.axis_index("col")
    deep = col // side
    across = col % side
    me = row * side + across
    rest = pl.ds(0, (plane - 1) * pad)

    def slot_of(other):
        return pl.ds(pl.multiple_of(other * pad, 8), pad)

    def peer_id(other):
        return (other // side, deep * side + other % side)

    def partner(j):
        if plane & (plane - 1):
            return (me + j) % plane
        return sum(bit * ((me // bit + j // bit) % 2) for bit in (1 << i for i in range(plane.bit_length() - 1)))

    def deep_id(step):
        return (row, flip(deep, step) * side + across)

    barrier = pltpu.get_barrier_semaphore()

    @pl.loop(1, plane)
    def _(j):
        pl.semaphore_signal(barrier, inc=1, device_id=peer_id((me + j) % plane), device_id_type=MESH)

    for step in range(1, DEEP):
        pl.semaphore_signal(barrier, inc=1, device_id=deep_id(step), device_id_type=MESH)

    weights = [pltpu.make_async_copy(src.at[0], dst, wsem.at[i])
               for i, (src, dst) in enumerate(((wg_hbm, wg), (wu_hbm, wu), (wd_hbm, wd)))]
    for copy in weights:
        copy.start()
    pl.semaphore_wait(barrier, plane - 1 + DEEP - 1)

    def tab_copy(step):
        return pltpu.make_async_remote_copy(
            tab_ref.at[flip(deep, step)], tabbuf.at[step - 1], tab_send.at[step], tab_recv.at[step],
            device_id=deep_id(step), device_id_type=MESH)

    def tok_copy(step):
        return pltpu.make_async_remote_copy(
            tok_ref, tokbuf.at[step - 1], tok_send.at[step], tok_recv.at[step],
            device_id=deep_id(step), device_id_type=MESH)

    def part_copy(step, piece):
        return pltpu.make_async_remote_copy(
            psend.at[step - 1, piece], precv.at[step - 1, piece], p_send.at[step, piece], p_recv.at[step, piece],
            device_id=deep_id(step), device_id_type=MESH)

    for step in range(1, DEEP):
        tab_copy(step).start()

    def wait_bytes(ref, sem):
        pltpu.make_async_copy(ref, ref, sem).wait()

    def table(step):
        return tab_ref[deep] if step == 0 else tabbuf[step - 1]

    slots = lax.broadcasted_iota(jnp.int32, (pad, tokens), 0).astype(jnp.float32)

    def pack(step):
        slot = step % 2
        if step:
            tab_copy(step).wait_recv()
            tok_copy(step).wait_recv()
            if step + 1 < DEEP:
                tok_copy(step + 1).start()
        if step >= 2:
            wait_bytes(stage.at[slot, rest], x_send.at[step - 2])
        tab = table(step)
        pick = jnp.concatenate(
            [jnp.where(slots == tab[p:p + 1, :], 1.0, 0.0) for p in range(plane)], axis=0
        ).astype(jnp.bfloat16)
        source = tok_ref if step == 0 else tokbuf.at[step - 1]

        @pl.loop(0, width // 512)
        def _(i):
            cols = pl.ds(pl.multiple_of(i * 512, 512), 512)
            packed = jnp.dot(pick, source[:, cols], preferred_element_type=jnp.float32)
            stage[slot, :, cols] = packed.astype(jnp.bfloat16)

        @pl.loop(1, plane)
        def _(j):
            other = partner(plane - j)
            pltpu.make_async_remote_copy(
                stage.at[slot, slot_of(other)], xbuf.at[step, slot_of(me)], x_send.at[step], x_recv.at[step],
                device_id=peer_id(other), device_id_type=MESH).start()

        pltpu.make_async_copy(stage.at[slot, slot_of(me)], xbuf.at[step, slot_of(me)], x_recv.at[step]).start()

    def expert(step):
        wait_bytes(xbuf.at[step], x_recv.at[step])
        if step == 0:
            weights[0].wait()
            weights[1].wait()

        @pl.loop(0, ffw // 256)
        def _(i):
            cols = pl.ds(pl.multiple_of(i * 256, 256), 256)
            arrived = xbuf[step]
            gate = jnp.dot(arrived, wg[:, cols], preferred_element_type=jnp.float32)
            up = jnp.dot(arrived, wu[:, cols], preferred_element_type=jnp.float32)
            hid[:, cols] = (gate / (1.0 + jnp.exp(-gate)) * up).astype(jnp.bfloat16)

        if step == 0:
            weights[2].wait()

        @pl.loop(0, width // 512)
        def _(i):
            cols = pl.ds(pl.multiple_of(i * 512, 512), 512)
            given = jnp.dot(hid[...], wd[:, cols], preferred_element_type=jnp.float32)
            xbuf[step, :, cols] = given.astype(jnp.bfloat16)

    def give_back(step):
        for piece in range(PIECES):
            cols = pl.ds(piece * part, part)

            @pl.loop(1, plane)
            def _(j):
                other = partner(plane - j)
                pltpu.make_async_remote_copy(
                    xbuf.at[step, slot_of(other), cols], back.at[step, piece, slot_of(me)],
                    r_send.at[step, piece], r_recv.at[step, piece],
                    device_id=peer_id(other), device_id_type=MESH).start()

            pltpu.make_async_copy(
                xbuf.at[step, slot_of(me), cols], back.at[step, piece, slot_of(me)], r_recv.at[step, piece]).start()

    def combine(step):
        tab = table(step)
        share = jnp.concatenate(
            [jnp.where(slots == tab[p:p + 1, :], tab[plane + p:plane + p + 1, :], 0.0) for p in range(plane)],
            axis=0).T
        high = share.astype(jnp.bfloat16)
        low = (share - high.astype(jnp.float32)).astype(jnp.bfloat16)
        for piece in range(PIECES):
            wait_bytes(back.at[step, piece], r_recv.at[step, piece])
            held = near.at[step, piece] if resident else near
            if not resident:
                load = pltpu.make_async_copy(far.at[step, piece], near, l_sem)
                load.start()
                load.wait()

            @pl.loop(0, part // 512)
            def _(i):
                cols = pl.ds(pl.multiple_of(i * 512, 512), 512)
                given = held[:, cols]
                total = jnp.dot(high, given, preferred_element_type=jnp.float32)
                total = total + jnp.dot(low, given, preferred_element_type=jnp.float32)
                if step == 0:
                    own[piece, :, cols] = total
                else:
                    psend[step - 1, piece, :, cols] = total.astype(jnp.bfloat16)

            if step:
                part_copy(step, piece).start()

    tok_copy(1).start()
    pack(0)
    pack(1)
    expert(0)
    pack(2)
    expert(1)
    give_back(1)
    pack(3)
    expert(2)
    give_back(2)
    expert(3)
    give_back(3)
    give_back(0)
    combine(1)
    combine(2)
    combine(3)
    combine(0)
    for piece in range(PIECES):
        for step in range(1, DEEP):
            part_copy(step, piece).wait_recv()

        @pl.loop(0, part // 512)
        def _(i):
            cols = pl.ds(pl.multiple_of(i * 512, 512), 512)
            whole = pl.ds(pl.multiple_of(piece * part + i * 512, 512), 512)
            total = own[piece, :, cols]
            for step in range(1, DEEP):
                total = total + precv[step - 1, piece, :, cols].astype(jnp.float32)
            out_ref[:, whole] = total.astype(jnp.bfloat16)

    for step in range(1, DEEP):
        tab_copy(step).wait_send()
        tok_copy(step).wait_send()
        for piece in range(PIECES):
            part_copy(step, piece).wait_send()
    for step in range(DEEP):
        if step >= DEEP - 2:
            wait_bytes(stage.at[step % 2, rest], x_send.at[step])
        for piece in range(PIECES):
            wait_bytes(back.at[step, piece, rest], r_send.at[step, piece])


def grid_kernel(pad, tok_hbm, ids_hbm, router_hbm, wg_hbm, wu_hbm, wd_hbm, out_hbm,
                ids_ref, router_ref, tab_ref, pair, tabs, stage, xbuf, hid, back, precv, zrecv, wg, wu, wd,
                wsem, tok_sem, own_sem, tab_send, tab_recv, z_send, z_recv,
                f_send, f_recv, e_send, e_recv, x_send, x_recv, r_send, r_recv,
                p_send, p_recv, q_send, q_recv, o_sem):
    tokens, width = tok_hbm.shape
    ffw = wg.shape[1]
    chunk = 2 * pad
    part = width // PIECES
    row = lax.axis_index("row")
    col = lax.axis_index("col")
    y, core = row // 2, row % 2
    z, x = col // 2, col % 2
    upper = z // 2
    middle = z * (3 - z) // 2
    inner = middle == 1
    f = y * (1 - core) + x * core
    l = x * (1 - core) + y * core
    order = (z, 1 - z + 4 * upper, 2 - upper, 3 - 3 * upper)
    onward = (None, 3 - z, 3 * upper, 3 * upper)

    def at(first, last, which, deep):
        return ((first * (1 - core) + last * core) * 2 + which, deep * 2 + last * (1 - core) + first * core)

    sibling = (y * 2 + 1 - core, col)
    twin = at(1 - f, l, core, z)
    mine = pl.ds(pl.multiple_of(f * tokens, tokens), tokens)
    other = pl.ds(pl.multiple_of((1 - f) * tokens, tokens), tokens)

    def chunk_at(slot):
        return pl.ds(pl.multiple_of(slot * chunk, 16), chunk)

    def send(src, dst, ssem, rsem, device):
        return pltpu.make_async_remote_copy(src, dst, ssem, rsem, device_id=device, device_id_type=MESH)

    def wait_bytes(ref, sem):
        pltpu.make_async_copy(ref, ref, sem).wait()

    barrier = pltpu.get_barrier_semaphore()

    def greet(device):
        pl.semaphore_signal(barrier, inc=1, device_id=device, device_id_type=MESH)

    greet(sibling)
    for which in range(2):
        greet((y * 2 + which, z * 2 + 1 - x))
        greet(((1 - y) * 2 + which, col))
    for j in range(1, DEEP):
        for g in range(2):
            greet(at((f + g) % 2, l, core, (z + j) % DEEP))

    weights = [pltpu.make_async_copy(src.at[0], dst, wsem.at[i])
               for i, (src, dst) in enumerate(((wg_hbm, wg), (wu_hbm, wu), (wd_hbm, wd)))]
    own_tok = pltpu.make_async_copy(tok_hbm, pair.at[z, mine], tok_sem.at[0])
    own_ids = pltpu.make_async_copy(ids_hbm, ids_ref, tok_sem.at[1])
    own_router = pltpu.make_async_copy(router_hbm, router_ref, tok_sem.at[2])
    for copy in (own_tok, own_ids, own_router):
        copy.start()
    pl.semaphore_wait(barrier, 5 + 2 * (DEEP - 1))

    early, late = pl.ds(0, CB), pl.ds(CB, width - CB)

    def early_copy():
        return send(tok_hbm.at[:, early], pair.at[z, mine, early], e_send, e_recv, twin)

    def first_copy(k):
        src = tok_hbm.at[:, late] if k == 0 else pair.at[order[k], mine, late]
        return send(src, pair.at[order[k], mine, late], f_send.at[k], f_recv.at[k], twin)

    bands = ((mine, late), (mine, early), (other, early))

    def line_copy(band, block, index, target):
        rows, cols = bands[band]
        ref = pair.at[block, rows, cols]
        src = tok_hbm.at[:, cols] if index < 2 and band < 2 else ref
        return send(src, ref, z_send.at[band, index], z_recv.at[band, block], (row, target * 2 + x))

    def from_here(band):
        line_copy(band, z, 0, order[1]).start()

        @pl.when(inner)
        def _():
            line_copy(band, z, 1, onward[1]).start()

    early_copy().start()
    from_here(0)
    for copy in weights:
        copy.start()
    own_tok.wait()
    own_ids.wait()
    own_router.wait()
    experts = router_ref.shape[0]
    logits = lax.dot_general(router_ref[...], pair[z, mine, :], (((1,), (1,)), ((), ())),
                             preferred_element_type=jnp.float32)
    number = lax.broadcasted_iota(jnp.int32, (experts, tokens), 0)
    count = sum(jnp.where(number == ids_ref[k:k + 1, :], 1.0, 0.0) for k in range(ids_ref.shape[0]))
    named = count > 0.5
    top = jnp.max(jnp.where(named, logits, -jnp.inf), axis=0, keepdims=True)
    scores = jnp.where(named, jnp.exp(jnp.where(named, logits - top, 0.0)), 0.0)
    gates = scores / jnp.sum(scores, axis=0, keepdims=True)
    before = jnp.where(lax.broadcasted_iota(jnp.int32, (tokens, tokens), 0)
                       < lax.broadcasted_iota(jnp.int32, (tokens, tokens), 1), 1.0, 0.0).astype(jnp.bfloat16)
    rank = jnp.dot(count.astype(jnp.bfloat16), before, preferred_element_type=jnp.float32)
    rank = jnp.where(named, rank + (pad * f).astype(jnp.float32), -1.0)
    for deep in range(DEEP):
        for who in range(2):
            straight = [((who * 2 + j % 2) * DEEP + deep) * 2 + j // 2 for j in range(4)]
            turned = [((j // 2 * 2 + j % 2) * DEEP + deep) * 2 + who for j in range(4)]
            tab_ref[deep, who] = jnp.where(
                core == 0,
                jnp.concatenate([v[e:e + 1] for v in (rank, gates) for e in straight], axis=0),
                jnp.concatenate([v[e:e + 1] for v in (rank, gates) for e in turned], axis=0))

    for j in range(DEEP):
        for g in range(2):
            if j or g:
                who, deep = (f + g) % 2, (z + j) % DEEP
                send(tab_ref.at[deep, who], tabs.at[z, f], tab_send.at[j, g], tab_recv.at[z, f],
                     at(who, l, core, deep)).start()
    tabs[z, f] = tab_ref[z, f]
    first_copy(0).start()
    from_here(1)
    early_copy().wait_recv()
    from_here(2)

    def fetch(band, k):
        line_copy(band, order[k], 2, order[1]).wait_recv()
        if band == 0:
            first_copy(k).start()

        @pl.when(inner)
        def _():
            line_copy(band, order[k], 1 + k, onward[k]).start()

    places = lax.broadcasted_iota(jnp.int32, (chunk, tokens), 0).astype(jnp.float32)
    peers = [(l, core, None), (l, 1 - core, sibling),
             (1 - l, 0, at(f, 1 - l, 0, z)), (1 - l, 1, at(f, 1 - l, 1, z))]
    far = pl.ds(0, 3 * chunk)

    kept, primed = set(), set()

    def wait_kept(k):
        if k not in kept:
            kept.add(k)
            keep = chunk_at(l * 2 + core)
            wait_bytes(xbuf.at[k, keep], own_sem.at[k])

    picks = {}

    def pick_of(k):
        block = order[k]
        if k == 0:
            wait_bytes(tabs.at[block, 1 - f], tab_recv.at[block, 1 - f])
        else:
            wait_bytes(tabs.at[block, 0], tab_recv.at[block, 0])
            wait_bytes(tabs.at[block, 1], tab_recv.at[block, 1])
        if k >= 2:
            wait_bytes(stage.at[k % 2, far], x_send.at[k - 2])
            wait_kept(k - 2)
        low_tab, high_tab = tabs[block, 0], tabs[block, 1]
        pick = jnp.concatenate(
            [jnp.concatenate([jnp.where(places == low_tab[j:j + 1, :], 1.0, 0.0),
                              jnp.where(places == high_tab[j:j + 1, :], 1.0, 0.0)], axis=1) for j in range(4)],
            axis=0).astype(jnp.bfloat16)
        return pick

    def pack(k, pieces):
        slot = k % 2
        block = order[k]
        if k not in picks:
            picks[k] = pick_of(k)
        pick = picks[k]
        if pieces == LATE:
            first_copy(k).wait_recv()
        for piece in pieces:

            @pl.loop(0, part // TILE)
            def _(i):
                cols = pl.ds(pl.multiple_of(piece * part + i * TILE, TILE), TILE)
                packed = jnp.dot(pick, pair[block, :, cols], preferred_element_type=jnp.float32)
                stage[slot, :, cols] = packed.astype(jnp.bfloat16)

            cols = pl.ds(piece * part, part)
            for last, which, device in reversed(peers):
                src = stage.at[slot, chunk_at(last * 2 + which), cols]
                dst = xbuf.at[k, chunk_at(core * 2 + l), cols]
                if device is None:
                    pltpu.make_async_copy(src, dst, own_sem.at[k]).start()
                else:
                    send(src, dst, x_send.at[k], x_recv.at[k], device).start()

    holders = [(core, l, None), (1 - core, f, sibling),
               (0, 1 - x, (y * 2, z * 2 + 1 - x)), (1, 1 - y, ((1 - y) * 2 + 1, col))]

    def give_back(k, piece):
        cols = pl.ds(piece * part, part)
        for which, last, device in reversed(holders):
            place = x * (1 - which) + y * which
            src = xbuf.at[k, chunk_at(which * 2 + last), cols]
            dst = back.at[k, chunk_at(place * 2 + core), cols]
            if device is None:
                pltpu.make_async_copy(src, dst, r_recv.at[k, piece]).start()
            else:
                send(src, dst, r_send.at[k, piece], r_recv.at[k, piece], device).start()

    def expert_in(k):
        wait_bytes(xbuf.at[k, far], x_recv.at[k])
        wait_kept(k)
        if len(primed) == 0:
            weights[0].wait()
            weights[1].wait()

        @pl.loop(0, ffw // UP)
        def _(i):
            cols = pl.ds(pl.multiple_of(i * UP, UP), UP)
            arrived = xbuf[k]
            gate = jnp.dot(arrived, wg[:, cols], preferred_element_type=jnp.float32)
            up = jnp.dot(arrived, wu[:, cols], preferred_element_type=jnp.float32)
            hid[:, cols] = (gate / (1.0 + jnp.exp(-gate)) * up).astype(jnp.bfloat16)

    def expert_out(k, give):
        if len(primed) == 0:
            weights[2].wait()
        primed.add(k)
        for piece in range(PIECES):

            @pl.loop(0, part // DOWN)
            def _(i):
                cols = pl.ds(pl.multiple_of(piece * part + i * DOWN, DOWN), DOWN)
                given = jnp.dot(hid[...], wd[:, cols], preferred_element_type=jnp.float32)
                xbuf[k, :, cols] = given.astype(jnp.bfloat16)

            if give:
                give_back(k, piece)

    def share(k, half):
        tab = tabs[order[k], half]
        whole = jnp.concatenate(
            [jnp.where(places == tab[j:j + 1, :], tab[4 + j:5 + j, :], 0.0) for j in range(4)], axis=0).T
        high = whole.astype(jnp.bfloat16)
        low = (whole - high.astype(jnp.float32)).astype(jnp.bfloat16)
        return jnp.concatenate([high, low], axis=0)

    def mixed_of(both, k, cols):
        total = jnp.dot(both, back[k, :, cols], preferred_element_type=jnp.float32)
        return total[:tokens] + total[tokens:]

    def twin_copy(k, piece):
        cols = pl.ds(piece * part, part)
        return send(pair.at[order[k], other, cols], precv.at[k, :, cols],
                    p_send.at[k, piece], p_recv.at[k, piece], twin)

    def home_copy(k, piece):
        cols = pl.ds(piece * part, part)
        place = 0 if k == 1 else middle + (1 - middle) * k
        target = order[1] if k == 1 else middle * order[k] + (1 - middle) * order[1]
        return send(pair.at[order[k], mine, cols], zrecv.at[place, :, cols],
                    q_send.at[k, piece], q_recv.at[place, piece], (row, target * 2 + x))

    def combine_other(k):
        both = share(k, 1 - f)
        for piece in range(PIECES):
            wait_bytes(back.at[k, :, pl.ds(piece * part, part)], r_recv.at[k, piece])
            if piece == 0:
                if k == 0:
                    line_copy(2, z, 0, order[1]).wait_send()

                @pl.when(inner)
                def _():
                    index = 1 + k
                    line_copy(2, order[k], index, onward[max(k, 1)]).wait_send()

            @pl.loop(0, part // TILE)
            def _(i):
                cols = pl.ds(pl.multiple_of(piece * part + i * TILE, TILE), TILE)
                pair[order[k], other, cols] = mixed_of(both, k, cols).astype(jnp.bfloat16)

            twin_copy(k, piece).start()

    def out_copy(piece):
        cols = pl.ds(piece * part, part)
        return pltpu.make_async_copy(pair.at[z, mine, cols], out_hbm.at[:, cols], o_sem.at[piece])

    def combine_own(k):
        both = share(k, f)
        if k:
            first_copy(k).wait_send()

            @pl.when(inner)
            def _():
                for band in range(2):
                    line_copy(band, order[k], 1 + k, onward[k]).wait_send()

        def add_up(piece, places, result):
            for place in places:
                wait_bytes(zrecv.at[place, :, pl.ds(piece * part, part)], q_recv.at[place, piece])

            @pl.loop(0, part // TILE)
            def _(i):
                cols = pl.ds(pl.multiple_of(piece * part + i * TILE, TILE), TILE)
                total = mixed_of(both, k, cols) + precv[k, :, cols].astype(jnp.float32)
                for place in places:
                    total = total + zrecv[place, :, cols].astype(jnp.float32)
                result[:, cols] = total.astype(jnp.bfloat16)

        for piece in range(PIECES):
            twin_copy(k, piece).wait_recv()
            result = pair.at[order[k], mine]
            if k == 0:
                add_up(piece, (0, 1), result)
                out_copy(piece).start()
                continue
            if k == 1:
                add_up(piece, (), result)
            else:

                @pl.when(inner)
                def _():
                    add_up(piece, (k,), result)

                @pl.when(jnp.logical_not(inner))
                def _():
                    add_up(piece, (), result)

            home_copy(k, piece).start()

    pack(0, EARLY)
    fetch(0, 1)
    pack(0, LATE)

    @pl.when(inner)
    def _():
        fetch(0, 2)


    @pl.when(inner)
    def _():
        fetch(1, 1)
        fetch(2, 1)

    pack(1, LATE)

    @pl.when(inner)
    def _():
        fetch(1, 2)
        fetch(2, 2)


    @pl.when(jnp.logical_not(inner))
    def _():
        fetch(1, 1)
        fetch(2, 1)

    pack(1, EARLY)

    @pl.when(jnp.logical_not(inner))
    def _():
        fetch(0, 2)

    expert_in(1)
    expert_out(1, True)
    expert_in(0)

    @pl.when(inner)
    def _():
        fetch(0, 3)

    combine_other(1)
    expert_out(0, False)
    pack(2, LATE)

    @pl.when(jnp.logical_not(inner))
    def _():
        fetch(1, 2)
        fetch(2, 2)

    pack(2, EARLY)

    @pl.when(jnp.logical_not(inner))
    def _():
        fetch(0, 3)

    pack(3, LATE)

    @pl.when(inner)
    def _():
        fetch(1, 3)
        fetch(2, 3)

    expert_in(2)

    @pl.when(jnp.logical_not(inner))
    def _():
        fetch(1, 3)
        fetch(2, 3)

    pack(3, EARLY)
    combine_own(1)
    expert_out(2, True)
    expert_in(3)
    expert_out(3, False)
    combine_other(2)
    for piece in range(PIECES):
        give_back(3, piece)
    combine_own(2)
    combine_other(3)
    for piece in range(PIECES):
        give_back(0, piece)
    combine_own(3)
    combine_other(0)
    combine_own(0)

    early_copy().wait_send()
    first_copy(0).wait_send()
    for band in range(2):
        line_copy(band, z, 0, order[1]).wait_send()

        @pl.when(inner)
        def _():
            line_copy(band, z, 1, onward[1]).wait_send()

    for j in range(DEEP):
        for g in range(2):
            if j or g:
                wait_bytes(tab_ref.at[j, g], tab_send.at[j, g])
    for k in (2, 3):
        wait_bytes(stage.at[k % 2, far], x_send.at[k])
    for k in range(DEEP):
        for piece in range(PIECES):
            if k == 0:
                out_copy(piece).wait()
            wait_bytes(back.at[k, far, pl.ds(piece * part, part)], r_send.at[k, piece])
            twin_copy(k, piece).wait_send()
            if k:
                home_copy(k, piece).wait_send()


def grid_call(tokens, expert_ids, router_weight, w_gate, w_up, w_down):
    tok_count, width = tokens.shape
    top_count = expert_ids.shape[1]
    experts = router_weight.shape[1]
    ffw = w_gate.shape[2]
    pad = tok_count * top_count * 5 // (4 * experts)
    anywhere = pl.BlockSpec(memory_space=pl.ANY)
    dma = pltpu.SemaphoreType.DMA
    return pl.pallas_call(
        functools.partial(grid_kernel, pad),
        out_shape=jax.ShapeDtypeStruct((tok_count, width), jnp.bfloat16),
        in_specs=[anywhere] * 6,
        out_specs=anywhere,
        scratch_shapes=[
            pltpu.VMEM((top_count, tok_count), jnp.int32),
            pltpu.VMEM((experts, width), jnp.bfloat16),
            pltpu.VMEM((DEEP, 2, 8, tok_count), jnp.float32),
            pltpu.VMEM((DEEP, 2 * tok_count, width), jnp.bfloat16),
            pltpu.VMEM((DEEP, 2, 8, tok_count), jnp.float32),
            pltpu.VMEM((2, 8 * pad, width), jnp.bfloat16),
            pltpu.VMEM((DEEP, 8 * pad, width), jnp.bfloat16),
            pltpu.VMEM((8 * pad, ffw), jnp.bfloat16),
            pltpu.VMEM((DEEP, 8 * pad, width), jnp.bfloat16),
            pltpu.VMEM((DEEP, tok_count, width), jnp.bfloat16),
            pltpu.VMEM((DEEP, tok_count, width), jnp.bfloat16),
            pltpu.VMEM(w_gate.shape[1:], jnp.bfloat16),
            pltpu.VMEM(w_up.shape[1:], jnp.bfloat16),
            pltpu.VMEM(w_down.shape[1:], jnp.bfloat16),
            dma((3,)), dma((3,)), dma((DEEP,)), dma((DEEP, 2)), dma((DEEP, 2)), dma((3, 5)), dma((3, DEEP)),
            dma((DEEP,)), dma((DEEP,)), dma, dma, dma((DEEP,)), dma((DEEP,)),
            dma((DEEP, PIECES)), dma((DEEP, PIECES)), dma((DEEP, PIECES)), dma((DEEP, PIECES)),
            dma((DEEP, PIECES)), dma((DEEP, PIECES)), dma((PIECES,)),
        ],
        compiler_params=pltpu.CompilerParams(
            collective_id=1, has_side_effects=True, vmem_limit_bytes=63 * 1024 * 1024),
    )(tokens, expert_ids.T, router_weight.T, w_gate, w_up, w_down)


def per_device(tokens, expert_ids, router_weight, w_gate, w_up, w_down):
    tok_count, width = tokens.shape
    top_count = expert_ids.shape[1]
    experts = router_weight.shape[1]
    ffw = w_gate.shape[2]
    rows_axis = lax.axis_size("row")
    cols_axis = lax.axis_size("col")
    side = cols_axis // DEEP
    plane = rows_axis * side
    cap = tok_count * top_count * 5 // (4 * experts)
    pad = -(-cap // 8) * 8

    if (rows_axis, cols_axis) == (4, 2 * DEEP):
        return grid_call(tokens, expert_ids, router_weight, w_gate, w_up, w_down)

    logits = jnp.dot(tokens, router_weight, preferred_element_type=jnp.float32)
    named = jnp.any(expert_ids[:, :, None] == jnp.arange(experts, dtype=jnp.int32)[None, None, :], axis=1)
    top = jnp.max(jnp.where(named, logits, -jnp.inf), axis=1, keepdims=True)
    scores = jnp.where(named, jnp.exp(jnp.where(named, logits - top, 0.0)), 0.0)
    gates = scores / jnp.sum(scores, axis=1, keepdims=True)
    before = jnp.tril(jnp.ones((tok_count, tok_count), jnp.bfloat16), -1)
    rank = jnp.dot(before, named.astype(jnp.bfloat16), preferred_element_type=jnp.float32)
    rank = jnp.where(named, rank, -1.0)
    both = jnp.stack([rank, gates]).reshape(2, tok_count, rows_axis, DEEP, side)
    tab = both.transpose(3, 0, 2, 4, 1).reshape(DEEP, 2 * plane, tok_count)

    vmem = pl.BlockSpec(memory_space=pltpu.VMEM)
    anywhere = pl.BlockSpec(memory_space=pl.ANY)
    dma = pltpu.SemaphoreType.DMA
    back_dims = (DEEP, PIECES, plane * pad, width // PIECES)
    resident = 4 * DEEP * plane * pad * width <= 24 * 1024 * 1024
    mixed = jax.ShapeDtypeStruct((tok_count, width), jnp.bfloat16)
    given = pl.pallas_call(
        functools.partial(moe_kernel, (rows_axis, side, pad, resident)),
        out_shape=(mixed,) if resident else (mixed, jax.ShapeDtypeStruct(back_dims, jnp.bfloat16)),
        in_specs=[vmem, vmem, anywhere, anywhere, anywhere],
        out_specs=(vmem,) if resident else (vmem, anywhere),
        scratch_shapes=[
            pltpu.VMEM((DEEP - 1, tok_count, width), jnp.bfloat16),
            pltpu.VMEM((DEEP - 1, 2 * plane, tok_count), jnp.float32),
            pltpu.VMEM((2, plane * pad, width), jnp.bfloat16),
            pltpu.VMEM((DEEP, plane * pad, width), jnp.bfloat16),
            pltpu.VMEM((plane * pad, ffw), jnp.bfloat16),
            pltpu.VMEM(back_dims if resident else back_dims[2:], jnp.bfloat16),
            pltpu.VMEM((DEEP - 1, PIECES, tok_count, width // PIECES), jnp.bfloat16),
            pltpu.VMEM((DEEP - 1, PIECES, tok_count, width // PIECES), jnp.bfloat16),
            pltpu.VMEM((PIECES, tok_count, width // PIECES), jnp.float32),
            pltpu.VMEM(w_gate.shape[1:], jnp.bfloat16),
            pltpu.VMEM(w_up.shape[1:], jnp.bfloat16),
            pltpu.VMEM(w_down.shape[1:], jnp.bfloat16),
            dma((3,)), dma((DEEP,)), dma((DEEP,)), dma((DEEP,)), dma((DEEP,)), dma((DEEP,)), dma((DEEP,)),
            dma((DEEP, PIECES)), dma((DEEP, PIECES)), dma((DEEP, PIECES)), dma((DEEP, PIECES)), dma,
        ],
        compiler_params=pltpu.CompilerParams(
            collective_id=0, has_side_effects=True, vmem_limit_bytes=63 * 1024 * 1024),
    )(tokens, tab, w_gate, w_up, w_down)
    return given[0]


def solution(mesh):
    placed = (
        P(("row", "col"), None),
        P(("row", "col"), None),
        P(),
        P(("row", "col"), None, None),
        P(("row", "col"), None, None),
        P(("row", "col"), None, None),
    )
    return jax.shard_map(
        per_device, mesh=mesh, in_specs=placed, out_specs=P(("row", "col"), None), check_vma=False
    )
```

```python
import functools

import jax
import jax.numpy as jnp
from jax import lax
from jax.experimental import pallas as pl
from jax.experimental.pallas import tpu as pltpu
from jax.sharding import PartitionSpec as P

MESH = pl.DeviceIdType.MESH
DEEP = 4
PIECES = 4
CB = 2048
UP = 256
DOWN = 512
TILE = 512
EARLY = range(CB * PIECES // 4096)
LATE = range(CB * PIECES // 4096, PIECES)


def flip(index, step):
    bit = step & 1
    if bit:
        index = index + 1 - 2 * (index % 2)
    if step & 2:
        index = index + 2 - 4 * ((index // 2) % 2)
    return index


def moe_kernel(dims, tok_ref, tab_ref, wg_hbm, wu_hbm, wd_hbm, out_ref, *refs):
    rows_axis, side, pad, resident = dims
    far = None if resident else refs[0]
    (tokbuf, tabbuf, stage, xbuf, hid, near, psend, precv, own, wg, wu, wd,
     wsem, tok_send, tok_recv, tab_send, tab_recv, x_send, x_recv,
     r_send, r_recv, p_send, p_recv, l_sem) = refs if resident else refs[1:]
    back = near if resident else far
    plane = rows_axis * side
    tokens, width = tok_ref.shape
    ffw = wg.shape[1]
    part = width // PIECES
    row = lax.axis_index("row")
    col = lax.axis_index("col")
    deep = col // side
    across = col % side
    me = row * side + across
    rest = pl.ds(0, (plane - 1) * pad)

    def slot_of(other):
        return pl.ds(pl.multiple_of(other * pad, 8), pad)

    def peer_id(other):
        return (other // side, deep * side + other % side)

    def partner(j):
        if plane & (plane - 1):
            return (me + j) % plane
        return sum(bit * ((me // bit + j // bit) % 2) for bit in (1 << i for i in range(plane.bit_length() - 1)))

    def deep_id(step):
        return (row, flip(deep, step) * side + across)

    barrier = pltpu.get_barrier_semaphore()

    @pl.loop(1, plane)
    def _(j):
        pl.semaphore_signal(barrier, inc=1, device_id=peer_id((me + j) % plane), device_id_type=MESH)

    for step in range(1, DEEP):
        pl.semaphore_signal(barrier, inc=1, device_id=deep_id(step), device_id_type=MESH)

    weights = [pltpu.make_async_copy(src.at[0], dst, wsem.at[i])
               for i, (src, dst) in enumerate(((wg_hbm, wg), (wu_hbm, wu), (wd_hbm, wd)))]
    for copy in weights:
        copy.start()
    pl.semaphore_wait(barrier, plane - 1 + DEEP - 1)

    def tab_copy(step):
        return pltpu.make_async_remote_copy(
            tab_ref.at[flip(deep, step)], tabbuf.at[step - 1], tab_send.at[step], tab_recv.at[step],
            device_id=deep_id(step), device_id_type=MESH)

    def tok_copy(step):
        return pltpu.make_async_remote_copy(
            tok_ref, tokbuf.at[step - 1], tok_send.at[step], tok_recv.at[step],
            device_id=deep_id(step), device_id_type=MESH)

    def part_copy(step, piece):
        return pltpu.make_async_remote_copy(
            psend.at[step - 1, piece], precv.at[step - 1, piece], p_send.at[step, piece], p_recv.at[step, piece],
            device_id=deep_id(step), device_id_type=MESH)

    for step in range(1, DEEP):
        tab_copy(step).start()

    def wait_bytes(ref, sem):
        pltpu.make_async_copy(ref, ref, sem).wait()

    def table(step):
        return tab_ref[deep] if step == 0 else tabbuf[step - 1]

    slots = lax.broadcasted_iota(jnp.int32, (pad, tokens), 0).astype(jnp.float32)

    def pack(step):
        slot = step % 2
        if step:
            tab_copy(step).wait_recv()
            tok_copy(step).wait_recv()
            if step + 1 < DEEP:
                tok_copy(step + 1).start()
        if step >= 2:
            wait_bytes(stage.at[slot, rest], x_send.at[step - 2])
        tab = table(step)
        pick = jnp.concatenate(
            [jnp.where(slots == tab[p:p + 1, :], 1.0, 0.0) for p in range(plane)], axis=0
        ).astype(jnp.bfloat16)
        source = tok_ref if step == 0 else tokbuf.at[step - 1]

        @pl.loop(0, width // 512)
        def _(i):
            cols = pl.ds(pl.multiple_of(i * 512, 512), 512)
            packed = jnp.dot(pick, source[:, cols], preferred_element_type=jnp.float32)
            stage[slot, :, cols] = packed.astype(jnp.bfloat16)

        @pl.loop(1, plane)
        def _(j):
            other = partner(plane - j)
            pltpu.make_async_remote_copy(
                stage.at[slot, slot_of(other)], xbuf.at[step, slot_of(me)], x_send.at[step], x_recv.at[step],
                device_id=peer_id(other), device_id_type=MESH).start()

        pltpu.make_async_copy(stage.at[slot, slot_of(me)], xbuf.at[step, slot_of(me)], x_recv.at[step]).start()

    def expert(step):
        wait_bytes(xbuf.at[step], x_recv.at[step])
        if step == 0:
            weights[0].wait()
            weights[1].wait()

        @pl.loop(0, ffw // 256)
        def _(i):
            cols = pl.ds(pl.multiple_of(i * 256, 256), 256)
            arrived = xbuf[step]
            gate = jnp.dot(arrived, wg[:, cols], preferred_element_type=jnp.float32)
            up = jnp.dot(arrived, wu[:, cols], preferred_element_type=jnp.float32)
            hid[:, cols] = (gate / (1.0 + jnp.exp(-gate)) * up).astype(jnp.bfloat16)

        if step == 0:
            weights[2].wait()

        @pl.loop(0, width // 512)
        def _(i):
            cols = pl.ds(pl.multiple_of(i * 512, 512), 512)
            given = jnp.dot(hid[...], wd[:, cols], preferred_element_type=jnp.float32)
            xbuf[step, :, cols] = given.astype(jnp.bfloat16)

    def give_back(step):
        for piece in range(PIECES):
            cols = pl.ds(piece * part, part)

            @pl.loop(1, plane)
            def _(j):
                other = partner(plane - j)
                pltpu.make_async_remote_copy(
                    xbuf.at[step, slot_of(other), cols], back.at[step, piece, slot_of(me)],
                    r_send.at[step, piece], r_recv.at[step, piece],
                    device_id=peer_id(other), device_id_type=MESH).start()

            pltpu.make_async_copy(
                xbuf.at[step, slot_of(me), cols], back.at[step, piece, slot_of(me)], r_recv.at[step, piece]).start()

    def combine(step):
        tab = table(step)
        share = jnp.concatenate(
            [jnp.where(slots == tab[p:p + 1, :], tab[plane + p:plane + p + 1, :], 0.0) for p in range(plane)],
            axis=0).T
        high = share.astype(jnp.bfloat16)
        low = (share - high.astype(jnp.float32)).astype(jnp.bfloat16)
        for piece in range(PIECES):
            wait_bytes(back.at[step, piece], r_recv.at[step, piece])
            held = near.at[step, piece] if resident else near
            if not resident:
                load = pltpu.make_async_copy(far.at[step, piece], near, l_sem)
                load.start()
                load.wait()

            @pl.loop(0, part // 512)
            def _(i):
                cols = pl.ds(pl.multiple_of(i * 512, 512), 512)
                given = held[:, cols]
                total = jnp.dot(high, given, preferred_element_type=jnp.float32)
                total = total + jnp.dot(low, given, preferred_element_type=jnp.float32)
                if step == 0:
                    own[piece, :, cols] = total
                else:
                    psend[step - 1, piece, :, cols] = total.astype(jnp.bfloat16)

            if step:
                part_copy(step, piece).start()

    tok_copy(1).start()
    pack(0)
    pack(1)
    expert(0)
    pack(2)
    expert(1)
    give_back(1)
    pack(3)
    expert(2)
    give_back(2)
    expert(3)
    give_back(3)
    give_back(0)
    combine(1)
    combine(2)
    combine(3)
    combine(0)
    for piece in range(PIECES):
        for step in range(1, DEEP):
            part_copy(step, piece).wait_recv()

        @pl.loop(0, part // 512)
        def _(i):
            cols = pl.ds(pl.multiple_of(i * 512, 512), 512)
            whole = pl.ds(pl.multiple_of(piece * part + i * 512, 512), 512)
            total = own[piece, :, cols]
            for step in range(1, DEEP):
                total = total + precv[step - 1, piece, :, cols].astype(jnp.float32)
            out_ref[:, whole] = total.astype(jnp.bfloat16)

    for step in range(1, DEEP):
        tab_copy(step).wait_send()
        tok_copy(step).wait_send()
        for piece in range(PIECES):
            part_copy(step, piece).wait_send()
    for step in range(DEEP):
        if step >= DEEP - 2:
            wait_bytes(stage.at[step % 2, rest], x_send.at[step])
        for piece in range(PIECES):
            wait_bytes(back.at[step, piece, rest], r_send.at[step, piece])


def grid_kernel(pad, tok_hbm, ids_hbm, router_hbm, wg_hbm, wu_hbm, wd_hbm, out_hbm,
                ids_ref, router_ref, tab_ref, pair, tabs, stage, xbuf, hid, back, precv, zrecv, wg, wu, wd,
                wsem, tok_sem, own_sem, tab_send, tab_recv, z_send, z_recv,
                f_send, f_recv, e_send, e_recv, x_send, x_recv, r_send, r_recv,
                p_send, p_recv, q_send, q_recv, o_sem):
    tokens, width = tok_hbm.shape
    ffw = wg.shape[1]
    chunk = 2 * pad
    part = width // PIECES
    row = lax.axis_index("row")
    col = lax.axis_index("col")
    y, core = row // 2, row % 2
    z, x = col // 2, col % 2
    upper = z // 2
    middle = z * (3 - z) // 2
    inner = middle == 1
    f = y * (1 - core) + x * core
    l = x * (1 - core) + y * core
    order = (z, 1 - z + 4 * upper, 2 - upper, 3 - 3 * upper)
    onward = (None, 3 - z, 3 * upper, 3 * upper)

    def at(first, last, which, deep):
        return ((first * (1 - core) + last * core) * 2 + which, deep * 2 + last * (1 - core) + first * core)

    sibling = (y * 2 + 1 - core, col)
    twin = at(1 - f, l, core, z)
    mine = pl.ds(pl.multiple_of(f * tokens, tokens), tokens)
    other = pl.ds(pl.multiple_of((1 - f) * tokens, tokens), tokens)

    def chunk_at(slot):
        return pl.ds(pl.multiple_of(slot * chunk, 16), chunk)

    def send(src, dst, ssem, rsem, device):
        return pltpu.make_async_remote_copy(src, dst, ssem, rsem, device_id=device, device_id_type=MESH)

    def wait_bytes(ref, sem):
        pltpu.make_async_copy(ref, ref, sem).wait()

    barrier = pltpu.get_barrier_semaphore()

    def greet(device):
        pl.semaphore_signal(barrier, inc=1, device_id=device, device_id_type=MESH)

    greet(sibling)
    for which in range(2):
        greet((y * 2 + which, z * 2 + 1 - x))
        greet(((1 - y) * 2 + which, col))
    for j in range(1, DEEP):
        for g in range(2):
            greet(at((f + g) % 2, l, core, (z + j) % DEEP))

    weights = [pltpu.make_async_copy(src.at[0], dst, wsem.at[i])
               for i, (src, dst) in enumerate(((wg_hbm, wg), (wu_hbm, wu), (wd_hbm, wd)))]
    own_tok = pltpu.make_async_copy(tok_hbm, pair.at[z, mine], tok_sem.at[0])
    own_ids = pltpu.make_async_copy(ids_hbm, ids_ref, tok_sem.at[1])
    own_router = pltpu.make_async_copy(router_hbm, router_ref, tok_sem.at[2])
    for copy in (own_tok, own_ids, own_router):
        copy.start()
    pl.semaphore_wait(barrier, 5 + 2 * (DEEP - 1))

    early, late = pl.ds(0, CB), pl.ds(CB, width - CB)

    def early_copy():
        return send(tok_hbm.at[:, early], pair.at[z, mine, early], e_send, e_recv, twin)

    def first_copy(k):
        src = tok_hbm.at[:, late] if k == 0 else pair.at[order[k], mine, late]
        return send(src, pair.at[order[k], mine, late], f_send.at[k], f_recv.at[k], twin)

    bands = ((mine, late), (mine, early), (other, early))

    def line_copy(band, block, index, target):
        rows, cols = bands[band]
        ref = pair.at[block, rows, cols]
        src = tok_hbm.at[:, cols] if index < 2 and band < 2 else ref
        return send(src, ref, z_send.at[band, index], z_recv.at[band, block], (row, target * 2 + x))

    def from_here(band):
        line_copy(band, z, 0, order[1]).start()

        @pl.when(inner)
        def _():
            line_copy(band, z, 1, onward[1]).start()

    early_copy().start()
    from_here(0)
    for copy in weights:
        copy.start()
    own_tok.wait()
    own_ids.wait()
    own_router.wait()
    experts = router_ref.shape[0]
    logits = lax.dot_general(router_ref[...], pair[z, mine, :], (((1,), (1,)), ((), ())),
                             preferred_element_type=jnp.float32)
    number = lax.broadcasted_iota(jnp.int32, (experts, tokens), 0)
    count = sum(jnp.where(number == ids_ref[k:k + 1, :], 1.0, 0.0) for k in range(ids_ref.shape[0]))
    named = count > 0.5
    top = jnp.max(jnp.where(named, logits, -jnp.inf), axis=0, keepdims=True)
    scores = jnp.where(named, jnp.exp(jnp.where(named, logits - top, 0.0)), 0.0)
    gates = scores / jnp.sum(scores, axis=0, keepdims=True)
    before = jnp.where(lax.broadcasted_iota(jnp.int32, (tokens, tokens), 0)
                       < lax.broadcasted_iota(jnp.int32, (tokens, tokens), 1), 1.0, 0.0).astype(jnp.bfloat16)
    rank = jnp.dot(count.astype(jnp.bfloat16), before, preferred_element_type=jnp.float32)
    rank = jnp.where(named, rank + (pad * f).astype(jnp.float32), -1.0)
    for deep in range(DEEP):
        for who in range(2):
            straight = [((who * 2 + j % 2) * DEEP + deep) * 2 + j // 2 for j in range(4)]
            turned = [((j // 2 * 2 + j % 2) * DEEP + deep) * 2 + who for j in range(4)]
            tab_ref[deep, who] = jnp.where(
                core == 0,
                jnp.concatenate([v[e:e + 1] for v in (rank, gates) for e in straight], axis=0),
                jnp.concatenate([v[e:e + 1] for v in (rank, gates) for e in turned], axis=0))

    for j in range(DEEP):
        for g in range(2):
            if j or g:
                who, deep = (f + g) % 2, (z + j) % DEEP
                send(tab_ref.at[deep, who], tabs.at[z, f], tab_send.at[j, g], tab_recv.at[z, f],
                     at(who, l, core, deep)).start()
    tabs[z, f] = tab_ref[z, f]
    first_copy(0).start()
    from_here(1)
    early_copy().wait_recv()
    from_here(2)

    def fetch(band, k):
        line_copy(band, order[k], 2, order[1]).wait_recv()
        if band == 0:
            first_copy(k).start()

        @pl.when(inner)
        def _():
            line_copy(band, order[k], 1 + k, onward[k]).start()

    places = lax.broadcasted_iota(jnp.int32, (chunk, tokens), 0).astype(jnp.float32)
    peers = [(l, core, None), (l, 1 - core, sibling),
             (1 - l, 0, at(f, 1 - l, 0, z)), (1 - l, 1, at(f, 1 - l, 1, z))]
    far = pl.ds(0, 3 * chunk)

    kept, primed = set(), set()

    def wait_kept(k):
        if k not in kept:
            kept.add(k)
            keep = chunk_at(l * 2 + core)
            wait_bytes(xbuf.at[k, keep], own_sem.at[k])

    picks = {}

    def pick_of(k):
        block = order[k]
        if k == 0:
            wait_bytes(tabs.at[block, 1 - f], tab_recv.at[block, 1 - f])
        else:
            wait_bytes(tabs.at[block, 0], tab_recv.at[block, 0])
            wait_bytes(tabs.at[block, 1], tab_recv.at[block, 1])
        if k >= 2:
            wait_bytes(stage.at[k % 2, far], x_send.at[k - 2])
            wait_kept(k - 2)
        low_tab, high_tab = tabs[block, 0], tabs[block, 1]
        pick = jnp.concatenate(
            [jnp.concatenate([jnp.where(places == low_tab[j:j + 1, :], 1.0, 0.0),
                              jnp.where(places == high_tab[j:j + 1, :], 1.0, 0.0)], axis=1) for j in range(4)],
            axis=0).astype(jnp.bfloat16)
        return pick

    def pack(k, pieces):
        slot = k % 2
        block = order[k]
        if k not in picks:
            picks[k] = pick_of(k)
        pick = picks[k]
        if pieces == LATE:
            first_copy(k).wait_recv()
        for piece in pieces:

            @pl.loop(0, part // TILE)
            def _(i):
                cols = pl.ds(pl.multiple_of(piece * part + i * TILE, TILE), TILE)
                packed = jnp.dot(pick, pair[block, :, cols], preferred_element_type=jnp.float32)
                stage[slot, :, cols] = packed.astype(jnp.bfloat16)

            cols = pl.ds(piece * part, part)
            for last, which, device in reversed(peers):
                src = stage.at[slot, chunk_at(last * 2 + which), cols]
                dst = xbuf.at[k, chunk_at(core * 2 + l), cols]
                if device is None:
                    pltpu.make_async_copy(src, dst, own_sem.at[k]).start()
                else:
                    send(src, dst, x_send.at[k], x_recv.at[k], device).start()

    holders = [(core, l, None), (1 - core, f, sibling),
               (0, 1 - x, (y * 2, z * 2 + 1 - x)), (1, 1 - y, ((1 - y) * 2 + 1, col))]

    def give_back(k, piece):
        cols = pl.ds(piece * part, part)
        for which, last, device in reversed(holders):
            place = x * (1 - which) + y * which
            src = xbuf.at[k, chunk_at(which * 2 + last), cols]
            dst = back.at[k, chunk_at(place * 2 + core), cols]
            if device is None:
                pltpu.make_async_copy(src, dst, r_recv.at[k, piece]).start()
            else:
                send(src, dst, r_send.at[k, piece], r_recv.at[k, piece], device).start()

    def expert_in(k):
        wait_bytes(xbuf.at[k, far], x_recv.at[k])
        wait_kept(k)
        if len(primed) == 0:
            weights[0].wait()
            weights[1].wait()

        @pl.loop(0, ffw // UP)
        def _(i):
            cols = pl.ds(pl.multiple_of(i * UP, UP), UP)
            arrived = xbuf[k]
            gate = jnp.dot(arrived, wg[:, cols], preferred_element_type=jnp.float32)
            up = jnp.dot(arrived, wu[:, cols], preferred_element_type=jnp.float32)
            hid[:, cols] = (gate / (1.0 + jnp.exp(-gate)) * up).astype(jnp.bfloat16)

    def expert_out(k, give):
        if len(primed) == 0:
            weights[2].wait()
        primed.add(k)
        for piece in range(PIECES):

            @pl.loop(0, part // DOWN)
            def _(i):
                cols = pl.ds(pl.multiple_of(piece * part + i * DOWN, DOWN), DOWN)
                given = jnp.dot(hid[...], wd[:, cols], preferred_element_type=jnp.float32)
                xbuf[k, :, cols] = given.astype(jnp.bfloat16)

            if give:
                give_back(k, piece)

    def share(k, half):
        tab = tabs[order[k], half]
        whole = jnp.concatenate(
            [jnp.where(places == tab[j:j + 1, :], tab[4 + j:5 + j, :], 0.0) for j in range(4)], axis=0).T
        high = whole.astype(jnp.bfloat16)
        low = (whole - high.astype(jnp.float32)).astype(jnp.bfloat16)
        return jnp.concatenate([high, low], axis=0)

    def mixed_of(both, k, cols):
        total = jnp.dot(both, back[k, :, cols], preferred_element_type=jnp.float32)
        return total[:tokens] + total[tokens:]

    def twin_copy(k, piece):
        cols = pl.ds(piece * part, part)
        return send(pair.at[order[k], other, cols], precv.at[k, :, cols],
                    p_send.at[k, piece], p_recv.at[k, piece], twin)

    def home_copy(k, piece):
        cols = pl.ds(piece * part, part)
        place = 0 if k == 1 else middle + (1 - middle) * k
        target = order[1] if k == 1 else middle * order[k] + (1 - middle) * order[1]
        return send(pair.at[order[k], mine, cols], zrecv.at[place, :, cols],
                    q_send.at[k, piece], q_recv.at[place, piece], (row, target * 2 + x))

    def combine_other(k):
        both = share(k, 1 - f)
        for piece in range(PIECES):
            wait_bytes(back.at[k, :, pl.ds(piece * part, part)], r_recv.at[k, piece])
            if piece == 0:
                if k == 0:
                    line_copy(2, z, 0, order[1]).wait_send()

                @pl.when(inner)
                def _():
                    index = 1 + k
                    line_copy(2, order[k], index, onward[max(k, 1)]).wait_send()

            @pl.loop(0, part // TILE)
            def _(i):
                cols = pl.ds(pl.multiple_of(piece * part + i * TILE, TILE), TILE)
                pair[order[k], other, cols] = mixed_of(both, k, cols).astype(jnp.bfloat16)

            twin_copy(k, piece).start()

    def out_copy(piece):
        cols = pl.ds(piece * part, part)
        return pltpu.make_async_copy(pair.at[z, mine, cols], out_hbm.at[:, cols], o_sem.at[piece])

    def combine_own(k):
        both = share(k, f)
        if k:
            first_copy(k).wait_send()

            @pl.when(inner)
            def _():
                for band in range(2):
                    line_copy(band, order[k], 1 + k, onward[k]).wait_send()

        def add_up(piece, places, result):
            for place in places:
                wait_bytes(zrecv.at[place, :, pl.ds(piece * part, part)], q_recv.at[place, piece])

            @pl.loop(0, part // TILE)
            def _(i):
                cols = pl.ds(pl.multiple_of(piece * part + i * TILE, TILE), TILE)
                total = mixed_of(both, k, cols) + precv[k, :, cols].astype(jnp.float32)
                for place in places:
                    total = total + zrecv[place, :, cols].astype(jnp.float32)
                result[:, cols] = total.astype(jnp.bfloat16)

        for piece in range(PIECES):
            twin_copy(k, piece).wait_recv()
            result = pair.at[order[k], mine]
            if k == 0:
                add_up(piece, (0, 1), result)
                out_copy(piece).start()
                continue
            if k == 1:
                add_up(piece, (), result)
            else:

                @pl.when(inner)
                def _():
                    add_up(piece, (k,), result)

                @pl.when(jnp.logical_not(inner))
                def _():
                    add_up(piece, (), result)

            home_copy(k, piece).start()

    pack(0, EARLY)
    fetch(0, 1)
    pack(0, LATE)

    @pl.when(inner)
    def _():
        fetch(0, 2)


    @pl.when(inner)
    def _():
        fetch(1, 1)
        fetch(2, 1)

    pack(1, LATE)

    @pl.when(jnp.logical_not(inner))
    def _():
        fetch(1, 1)
        fetch(2, 1)


    @pl.when(inner)
    def _():
        fetch(1, 2)
        fetch(2, 2)

    pack(1, EARLY)

    @pl.when(jnp.logical_not(inner))
    def _():
        fetch(0, 2)

    expert_in(1)
    expert_out(1, True)
    expert_in(0)

    @pl.when(inner)
    def _():
        fetch(0, 3)

    combine_other(1)
    expert_out(0, False)
    pack(2, LATE)

    @pl.when(jnp.logical_not(inner))
    def _():
        fetch(1, 2)
        fetch(2, 2)


    @pl.when(inner)
    def _():
        fetch(1, 3)
        fetch(2, 3)

    pack(2, EARLY)

    @pl.when(jnp.logical_not(inner))
    def _():
        fetch(0, 3)

    pack(3, LATE)
    expert_in(2)

    @pl.when(jnp.logical_not(inner))
    def _():
        fetch(1, 3)
        fetch(2, 3)

    pack(3, EARLY)
    combine_own(1)
    expert_out(2, True)
    expert_in(3)
    expert_out(3, False)
    combine_other(2)
    for piece in range(PIECES):
        give_back(3, piece)
    combine_own(2)
    combine_other(3)
    for piece in range(PIECES):
        give_back(0, piece)
    combine_own(3)
    combine_other(0)
    combine_own(0)

    early_copy().wait_send()
    first_copy(0).wait_send()
    for band in range(2):
        line_copy(band, z, 0, order[1]).wait_send()

        @pl.when(inner)
        def _():
            line_copy(band, z, 1, onward[1]).wait_send()

    for j in range(DEEP):
        for g in range(2):
            if j or g:
                wait_bytes(tab_ref.at[j, g], tab_send.at[j, g])
    for k in (2, 3):
        wait_bytes(stage.at[k % 2, far], x_send.at[k])
    for k in range(DEEP):
        for piece in range(PIECES):
            if k == 0:
                out_copy(piece).wait()
            wait_bytes(back.at[k, far, pl.ds(piece * part, part)], r_send.at[k, piece])
            twin_copy(k, piece).wait_send()
            if k:
                home_copy(k, piece).wait_send()


def grid_call(tokens, expert_ids, router_weight, w_gate, w_up, w_down):
    tok_count, width = tokens.shape
    top_count = expert_ids.shape[1]
    experts = router_weight.shape[1]
    ffw = w_gate.shape[2]
    pad = tok_count * top_count * 5 // (4 * experts)
    anywhere = pl.BlockSpec(memory_space=pl.ANY)
    dma = pltpu.SemaphoreType.DMA
    return pl.pallas_call(
        functools.partial(grid_kernel, pad),
        out_shape=jax.ShapeDtypeStruct((tok_count, width), jnp.bfloat16),
        in_specs=[anywhere] * 6,
        out_specs=anywhere,
        scratch_shapes=[
            pltpu.VMEM((top_count, tok_count), jnp.int32),
            pltpu.VMEM((experts, width), jnp.bfloat16),
            pltpu.VMEM((DEEP, 2, 8, tok_count), jnp.float32),
            pltpu.VMEM((DEEP, 2 * tok_count, width), jnp.bfloat16),
            pltpu.VMEM((DEEP, 2, 8, tok_count), jnp.float32),
            pltpu.VMEM((2, 8 * pad, width), jnp.bfloat16),
            pltpu.VMEM((DEEP, 8 * pad, width), jnp.bfloat16),
            pltpu.VMEM((8 * pad, ffw), jnp.bfloat16),
            pltpu.VMEM((DEEP, 8 * pad, width), jnp.bfloat16),
            pltpu.VMEM((DEEP, tok_count, width), jnp.bfloat16),
            pltpu.VMEM((DEEP, tok_count, width), jnp.bfloat16),
            pltpu.VMEM(w_gate.shape[1:], jnp.bfloat16),
            pltpu.VMEM(w_up.shape[1:], jnp.bfloat16),
            pltpu.VMEM(w_down.shape[1:], jnp.bfloat16),
            dma((3,)), dma((3,)), dma((DEEP,)), dma((DEEP, 2)), dma((DEEP, 2)), dma((3, 5)), dma((3, DEEP)),
            dma((DEEP,)), dma((DEEP,)), dma, dma, dma((DEEP,)), dma((DEEP,)),
            dma((DEEP, PIECES)), dma((DEEP, PIECES)), dma((DEEP, PIECES)), dma((DEEP, PIECES)),
            dma((DEEP, PIECES)), dma((DEEP, PIECES)), dma((PIECES,)),
        ],
        compiler_params=pltpu.CompilerParams(
            collective_id=1, has_side_effects=True, vmem_limit_bytes=63 * 1024 * 1024),
    )(tokens, expert_ids.T, router_weight.T, w_gate, w_up, w_down)


def per_device(tokens, expert_ids, router_weight, w_gate, w_up, w_down):
    tok_count, width = tokens.shape
    top_count = expert_ids.shape[1]
    experts = router_weight.shape[1]
    ffw = w_gate.shape[2]
    rows_axis = lax.axis_size("row")
    cols_axis = lax.axis_size("col")
    side = cols_axis // DEEP
    plane = rows_axis * side
    cap = tok_count * top_count * 5 // (4 * experts)
    pad = -(-cap // 8) * 8

    if (rows_axis, cols_axis) == (4, 2 * DEEP):
        return grid_call(tokens, expert_ids, router_weight, w_gate, w_up, w_down)

    logits = jnp.dot(tokens, router_weight, preferred_element_type=jnp.float32)
    named = jnp.any(expert_ids[:, :, None] == jnp.arange(experts, dtype=jnp.int32)[None, None, :], axis=1)
    top = jnp.max(jnp.where(named, logits, -jnp.inf), axis=1, keepdims=True)
    scores = jnp.where(named, jnp.exp(jnp.where(named, logits - top, 0.0)), 0.0)
    gates = scores / jnp.sum(scores, axis=1, keepdims=True)
    before = jnp.tril(jnp.ones((tok_count, tok_count), jnp.bfloat16), -1)
    rank = jnp.dot(before, named.astype(jnp.bfloat16), preferred_element_type=jnp.float32)
    rank = jnp.where(named, rank, -1.0)
    both = jnp.stack([rank, gates]).reshape(2, tok_count, rows_axis, DEEP, side)
    tab = both.transpose(3, 0, 2, 4, 1).reshape(DEEP, 2 * plane, tok_count)

    vmem = pl.BlockSpec(memory_space=pltpu.VMEM)
    anywhere = pl.BlockSpec(memory_space=pl.ANY)
    dma = pltpu.SemaphoreType.DMA
    back_dims = (DEEP, PIECES, plane * pad, width // PIECES)
    resident = 4 * DEEP * plane * pad * width <= 24 * 1024 * 1024
    mixed = jax.ShapeDtypeStruct((tok_count, width), jnp.bfloat16)
    given = pl.pallas_call(
        functools.partial(moe_kernel, (rows_axis, side, pad, resident)),
        out_shape=(mixed,) if resident else (mixed, jax.ShapeDtypeStruct(back_dims, jnp.bfloat16)),
        in_specs=[vmem, vmem, anywhere, anywhere, anywhere],
        out_specs=(vmem,) if resident else (vmem, anywhere),
        scratch_shapes=[
            pltpu.VMEM((DEEP - 1, tok_count, width), jnp.bfloat16),
            pltpu.VMEM((DEEP - 1, 2 * plane, tok_count), jnp.float32),
            pltpu.VMEM((2, plane * pad, width), jnp.bfloat16),
            pltpu.VMEM((DEEP, plane * pad, width), jnp.bfloat16),
            pltpu.VMEM((plane * pad, ffw), jnp.bfloat16),
            pltpu.VMEM(back_dims if resident else back_dims[2:], jnp.bfloat16),
            pltpu.VMEM((DEEP - 1, PIECES, tok_count, width // PIECES), jnp.bfloat16),
            pltpu.VMEM((DEEP - 1, PIECES, tok_count, width // PIECES), jnp.bfloat16),
            pltpu.VMEM((PIECES, tok_count, width // PIECES), jnp.float32),
            pltpu.VMEM(w_gate.shape[1:], jnp.bfloat16),
            pltpu.VMEM(w_up.shape[1:], jnp.bfloat16),
            pltpu.VMEM(w_down.shape[1:], jnp.bfloat16),
            dma((3,)), dma((DEEP,)), dma((DEEP,)), dma((DEEP,)), dma((DEEP,)), dma((DEEP,)), dma((DEEP,)),
            dma((DEEP, PIECES)), dma((DEEP, PIECES)), dma((DEEP, PIECES)), dma((DEEP, PIECES)), dma,
        ],
        compiler_params=pltpu.CompilerParams(
            collective_id=0, has_side_effects=True, vmem_limit_bytes=63 * 1024 * 1024),
    )(tokens, tab, w_gate, w_up, w_down)
    return given[0]


def solution(mesh):
    placed = (
        P(("row", "col"), None),
        P(("row", "col"), None),
        P(),
        P(("row", "col"), None, None),
        P(("row", "col"), None, None),
        P(("row", "col"), None, None),
    )
    return jax.shard_map(
        per_device, mesh=mesh, in_specs=placed, out_specs=P(("row", "col"), None), check_vma=False
    )
```
